32 devices in a mesh: mem: 8 (over z, x), fsdp: 4 (over y, core).
Axes of the slice: x: 2, y: 2, z: 4, core: 2. Of those that a mesh axis runs over, the one named last changes fastest.
Arguments:
- layer_input: bfloat16 [4096, 4096], P(('mem', 'fsdp')), may hold values from -6 to 6
- w_query: bfloat16 [4096, 2048], P('mem', 'fsdp'), may hold values from -0.09375 to 0.09375
- local_kv: bfloat16 [2, 4096, 2048], P(None, 'mem', 'fsdp'), may hold values from -200 to 200, as said below
- memory_kv: bfloat16 [128, 2, 128, 2048], P('mem', None, None, 'fsdp'), may hold values from -200 to 200
- memory_ids: int32 [32, 4], P('mem'), may hold values from 0 to 127, as said below
- grad_out: bfloat16 [4096, 2048], P('mem', 'fsdp'), may hold values from -6 to 6
Outputs:
- attended: bfloat16 [4096, 2048], P('mem', 'fsdp')
- grad_input: bfloat16 [4096, 4096], P(('mem', 'fsdp'))
The draws below stay inside these ranges and needn't reach their ends.
Inputs may be any that keep to these rules, and one draw needn't show every extreme that they name: `memory_ids`: within the tiles of one local context (4 tiles), all named blocks of one owner (same id // 16) are one and the same block, and every owner is named by some tile of every local context; each tile names 4 blocks of different owners. `local_kv`: keys and values of the document's tokens.
All inputs are finite; a program needn't handle non-finite values.
Results may differ from the reference program's by a relative error of at most 0.025.
The reference program's roundings to bfloat16 on the way count: a program that leaves them out, or rounds other values in their place, can miss the bound.
Values may be sent and summed in bfloat16 or wider, within the bound.
A program may use at most 128 MiB of HBM per device.

```python
import math
import jax
import jax.numpy as jnp
from jax import lax

D = 4096
HD = 128
BLK = 128
TOPK = 4
MB_DEV = 16
HW = 2048
CTX = 512
LEN = 4096
TILES = 32
MEMBLK = 128
N_FSDP = 4


def key_rows(key, rows_count, width):
    first_key = jax.random.fold_in(key, 0)
    return jnp.clip(jax.random.normal(first_key, (rows_count, width), jnp.float32), -4.0, 4.0)


def value_rows(key, rows_count, width):
    return jnp.clip(jax.random.normal(key, (rows_count, width), jnp.float32), -4.0, 4.0)


def draw_local_kv(key, part):
    keys_part = key_rows(jax.random.fold_in(key, 11), LEN, HW)
    values_part = value_rows(jax.random.fold_in(key, 12), LEN, HW)
    return jnp.stack([keys_part, values_part]).astype(jnp.bfloat16)


def draw_memory_kv(key, part):
    keys_part = key_rows(jax.random.fold_in(key, 21), MEMBLK * BLK, HW).reshape(MEMBLK, BLK, HW)
    values_part = value_rows(jax.random.fold_in(key, 22), MEMBLK * BLK, HW).reshape(MEMBLK, BLK, HW)
    return jnp.stack([keys_part, values_part], axis=1).astype(jnp.bfloat16)


def draw_memory_ids(key, part):
    owners_count = MEMBLK // MB_DEV
    groups = LEN // CTX
    tiles_per_group = CTX // BLK
    slots_count = tiles_per_group * TOPK
    first_key, second_key, third_key = jax.random.split(jax.random.fold_in(key, 31), 3)
    local_pick = jax.random.randint(first_key, (groups, owners_count), 0, MB_DEV)
    group_keys = jax.random.split(second_key, groups)
    orders = jax.vmap(lambda one_key: jax.random.permutation(one_key, owners_count))(group_keys).astype(jnp.int32)
    rotation = jax.random.randint(third_key, (groups, 1), 0, owners_count)
    slot_index = jnp.arange(slots_count, dtype=jnp.int32)
    positions = (slot_index[None, :] + rotation) % owners_count
    owners = jnp.take_along_axis(orders, positions, axis=1)
    local_part = jnp.take_along_axis(local_pick, owners, axis=1)
    block_ids = owners * MB_DEV + local_part
    return block_ids.reshape(TILES, TOPK).astype(jnp.int32)


def block_scale(own_key, shape, cuts, smallest, top_value):
    level, own = 1.0, jax.random.fold_in(own_key, 6)
    for position, parts in cuts:
        steps = jnp.exp(jax.random.uniform(jax.random.fold_in(own, position), (parts,), jnp.float32, smallest / len(cuts), top_value / len(cuts)))
        level = level * jnp.repeat(steps, shape[position] // parts).reshape([-1 if axis == position else 1 for axis in range(len(shape))])
    return level


def centred(own_key, extent, spread, most, cuts=(), kind=jnp.bfloat16):
    factor_of = block_scale(own_key, extent, cuts, -0.22, 0.18) if cuts else 1.0
    drawn = jax.random.normal(own_key, extent, jnp.float32) * spread * factor_of
    return jnp.minimum(jnp.maximum(drawn, -most), most).astype(kind)


def setup_inputs(seed: int = 0) -> dict:
    key_of = jax.random.split(jax.random.key(seed), 7)
    layer_input = centred(key_of[0], (LEN, D), 1.0, 6.0, ((0, 32),))
    w_query = centred(key_of[1], (D, HW), D ** -0.5, 0.09375, ((0, 8), (1, 4)))
    local_kv = draw_local_kv(jax.random.fold_in(key_of[6], 71), 0)
    memory_kv = draw_memory_kv(jax.random.fold_in(key_of[6], 71), 0)
    memory_ids = draw_memory_ids(jax.random.fold_in(key_of[6], 71), 0)
    grad_out = centred(key_of[5], (LEN, HW), 1.0, 6.0, ((0, 8), (1, 4)))
    return dict(layer_input=layer_input, w_query=w_query, local_kv=local_kv, memory_kv=memory_kv, memory_ids=memory_ids, grad_out=grad_out)


NEG_FILL = -1e+30

def attend_context(queries, context_kv, tile_kv, grad_rows):
    ctx_len, width = queries.shape
    heads_count = width // HD
    tiles_count = tile_kv.shape[0]
    mem_keys_count = TOPK * BLK
    score_scale = 1.0 / math.sqrt(HD)
    query_heads = queries.astype(jnp.float32).reshape(ctx_len, heads_count, HD)
    query_tiles = query_heads.reshape(tiles_count, BLK, heads_count, HD)
    local_keys = context_kv[0].astype(jnp.float32).reshape(ctx_len, heads_count, HD)
    local_values = context_kv[1].astype(jnp.float32).reshape(ctx_len, heads_count, HD)
    mem_keys = tile_kv[:, :, 0].astype(jnp.float32).reshape(tiles_count, mem_keys_count, heads_count, HD)
    mem_values = tile_kv[:, :, 1].astype(jnp.float32).reshape(tiles_count, mem_keys_count, heads_count, HD)
    grad_heads = grad_rows.astype(jnp.float32).reshape(ctx_len, heads_count, HD)
    grad_tiles = grad_heads.reshape(tiles_count, BLK, heads_count, HD)
    mem_scores = jnp.einsum('tqhd,tkhd->htqk', query_tiles, mem_keys) * score_scale
    mem_scores = mem_scores.reshape(heads_count, ctx_len, mem_keys_count)
    loc_scores = jnp.einsum('qhd,khd->hqk', query_heads, local_keys) * score_scale
    positions = jnp.arange(ctx_len, dtype=jnp.int32)
    causal = positions[:, None] >= positions[None, :]
    loc_scores = jnp.where(causal[None], loc_scores, NEG_FILL)
    row_max = jnp.maximum(lax.optimization_barrier(jnp.max(mem_scores, axis=2)), lax.optimization_barrier(jnp.max(loc_scores, axis=2)))
    mem_exp = jnp.exp(mem_scores - row_max[:, :, None])
    loc_exp = jnp.exp(loc_scores - row_max[:, :, None])
    total = lax.optimization_barrier(jnp.sum(mem_exp, axis=2)) + lax.optimization_barrier(jnp.sum(loc_exp, axis=2))
    mem_prob = mem_exp / total[:, :, None]
    loc_prob = loc_exp / total[:, :, None]
    mem_weights = lax.optimization_barrier(mem_prob.astype(jnp.bfloat16)).astype(jnp.float32)
    loc_weights = lax.optimization_barrier(loc_prob.astype(jnp.bfloat16)).astype(jnp.float32)
    mem_part = jnp.einsum('htqk,tkhd->tqhd', mem_weights.reshape(heads_count, tiles_count, BLK, mem_keys_count), mem_values)
    loc_part = jnp.einsum('hqk,khd->qhd', loc_weights, local_values)
    attended = (mem_part.reshape(ctx_len, heads_count, HD) + loc_part).reshape(ctx_len, width).astype(jnp.bfloat16)
    mem_dprob = jnp.einsum('tqhd,tkhd->htqk', grad_tiles, mem_values).reshape(heads_count, ctx_len, mem_keys_count)
    loc_dprob = jnp.einsum('qhd,khd->hqk', grad_heads, local_values)
    delta = lax.optimization_barrier(jnp.sum(mem_prob * mem_dprob, axis=2)) + lax.optimization_barrier(jnp.sum(loc_prob * loc_dprob, axis=2))
    mem_dscore = (mem_prob * (mem_dprob - delta[:, :, None])).astype(jnp.bfloat16)
    loc_dscore = (loc_prob * (loc_dprob - delta[:, :, None])).astype(jnp.bfloat16)
    mem_dscore = lax.optimization_barrier(mem_dscore).astype(jnp.float32)
    loc_dscore = lax.optimization_barrier(loc_dscore).astype(jnp.float32)
    mem_grad = jnp.einsum('htqk,tkhd->tqhd', mem_dscore.reshape(heads_count, tiles_count, BLK, mem_keys_count), mem_keys)
    loc_grad = jnp.einsum('hqk,khd->qhd', loc_dscore, local_keys)
    grad_queries = ((mem_grad.reshape(ctx_len, heads_count, HD) + loc_grad) * score_scale).reshape(ctx_len, width)
    return (attended, grad_queries.astype(jnp.bfloat16))

def reference(layer_input, w_query, local_kv, memory_kv, memory_ids, grad_out):
    queries = jnp.dot(layer_input, w_query, preferred_element_type=jnp.float32).astype(jnp.bfloat16)
    tiles_per_context = CTX // BLK

    def one_context(context_index):
        row_first = (context_index * CTX).astype(jnp.int32)
        tile_first = (context_index * tiles_per_context).astype(jnp.int32)
        query_rows = lax.dynamic_slice_in_dim(queries, row_first, CTX, 0)
        context_kv = lax.dynamic_slice_in_dim(local_kv, row_first, CTX, 1)
        grad_rows = lax.dynamic_slice_in_dim(grad_out, row_first, CTX, 0)
        block_ids = lax.dynamic_slice_in_dim(memory_ids, tile_first, tiles_per_context, 0)
        tile_kv = jnp.take(memory_kv, block_ids, axis=0)
        return attend_context(query_rows, context_kv, tile_kv, grad_rows)
    attended, grad_queries = lax.map(one_context, jnp.arange(LEN // CTX, dtype=jnp.int32))
    attended = attended.reshape(LEN, HW)
    grad_queries = grad_queries.reshape(LEN, HW)
    group_cols = HW // N_FSDP
    grad_total = jnp.zeros((LEN, D), jnp.float32)
    for group in range(N_FSDP):
        grad_cols = grad_queries[:, group * group_cols:(group + 1) * group_cols]
        weight_cols = w_query[:, group * group_cols:(group + 1) * group_cols]
        partial_sum = lax.dot_general(grad_cols, weight_cols, (((1,), (1,)), ((), ())), preferred_element_type=jnp.float32)
        grad_total = grad_total + lax.optimization_barrier(partial_sum.astype(jnp.bfloat16)).astype(jnp.float32)
    return (attended, grad_total.astype(jnp.bfloat16))
```

```python
import functools
import math

import jax
import jax.numpy as jnp
from jax import lax
from jax.experimental import pallas as pl
from jax.experimental.pallas import tpu as pltpu
from jax.sharding import PartitionSpec as P

HD = 128
BLK = 128
NEG_FILL = -1e30
MESH = pl.DeviceIdType.MESH
NT = (((1,), (1,)), ((), ()))


def dot_nn(a, b):
    return jnp.dot(a, b, preferred_element_type=jnp.float32)


def dot_nt(a, b):
    return lax.dot_general(a, b, NT, preferred_element_type=jnp.float32)


def kernel(
    n, nx, nf, mb_dev, early, per,
    ids_s, ids_v, x_hbm, w_hbm, lkv_hbm, mkv_hbm, go_hbm,
    att_ref, gin_ref,
    wf, xf, kv, lkv, go, outbox, inbox, stage, ids_in, ids_sm, q32, qb, gq,
    part, s_recv, y_send, y_recv, wy, gq_in,
    l_sem, i_send, i_recv, i_loc, w_up, w_down, w_x, w_recv, wx_recv,
    x_ysend, x_ssend, x_recv, m_send, m_recv, r_ssend, r_srecv, r_ysend, r_yrecv,
    v_ysend, v_ssend, v_recv, g_send, g_recv,
):
    me = lax.axis_index("mem")
    mf = lax.axis_index("fsdp")
    nz = n // nx
    z, xx = me // nx, lax.rem(me, nx)
    ny = nf // 2
    yy, cc = mf // 2, lax.rem(mf, 2)
    sib = mf + 1 - 2 * cc
    dk = wf.shape[1]
    width = wf.shape[2]
    heads = width // HD
    tiles, topk = ids_s.shape
    rows_dev = xf.shape[0] // nf
    late = early * HD

    def local_copy(src, dst, k):
        return pltpu.make_async_copy(src, dst, l_sem.at[k])

    def rows_of(f):
        return pl.ds(pl.multiple_of(f * rows_dev, rows_dev), rows_dev)

    c_w = local_copy(w_hbm, wf.at[me], 0)
    c_x = local_copy(x_hbm, xf.at[rows_of(mf), :], 1)
    c_kv = local_copy(mkv_hbm, kv, 2)
    c_lkv = local_copy(lkv_hbm, lkv, 3)
    c_go = local_copy(go_hbm, go, 4)
    c_w.start()
    c_x.start()
    c_kv.start()
    c_lkv.start()
    c_go.start()

    barrier = pltpu.get_barrier_semaphore()

    @pl.loop(1, n)
    def _(d):
        pl.semaphore_signal(
            barrier, inc=1, device_id=(lax.rem(me + d, n), mf), device_id_type=MESH
        )

    for d in range(1, nf):
        pl.semaphore_signal(
            barrier, inc=1, device_id=(me, lax.rem(mf + d, nf)), device_id_type=MESH
        )
    pl.semaphore_wait(barrier, n - 1 + nf - 1)

    def remote(src, dst, s, r, dm, df):
        return pltpu.make_async_remote_copy(
            src_ref=src, dst_ref=dst, send_sem=s, recv_sem=r,
            device_id=(dm, df), device_id_type=MESH,
        )

    def id_copy(peer, slot):
        return remote(ids_v, inbox.at[slot], i_send.at[peer], i_recv.at[slot], peer, mf)

    @pl.loop(1, n)
    def _(d):
        id_copy(lax.rem(me + d, n), me).start()

    def w_copy(slot, sem, dst_m, rsem):
        return remote(wf.at[slot], wf.at[slot], sem, rsem, dst_m, mf)

    def w_up_copy(zz):
        return w_copy(zz * nx + xx, w_up.at[zz], me + nx, w_recv.at[zz])

    def w_down_copy(zz):
        return w_copy(zz * nx + xx, w_down.at[zz], me - nx, w_recv.at[zz])

    x_next = z * nx + lax.rem(xx + 1, nx)

    def w_x_copy(r, zz):
        slot = zz * nx + lax.rem(xx - r + nx, nx)
        return w_copy(slot, w_x.at[r, zz], x_next, wx_recv.at[r, zz])

    def w_x_arrival(r, zz):
        slot = zz * nx + lax.rem(xx - 1 - r + 2 * nx, nx)
        return w_copy(slot, w_x.at[r, zz], x_next, wx_recv.at[r, zz])

    late_cols = slice(late, width)

    def v_ycopy(d, zz):
        return remote(
            wf.at[zz * nx + xx, :, late_cols], wy.at[mf, zz],
            v_ysend.at[d, zz], v_recv.at[mf, zz], me, lax.rem(mf + 2 * d, nf),
        )

    def v_own(zz):
        return remote(
            wf.at[zz * nx + xx, :, late_cols], wy.at[mf, zz],
            v_ssend.at[mf, zz], v_recv.at[mf, zz], me, sib,
        )

    def v_fwd(f, zz):
        return remote(
            wy.at[f, zz], wy.at[f, zz], v_ssend.at[f, zz], v_recv.at[f, zz], me, sib
        )

    def v_start(zz):
        for d in range(1, ny):
            v_ycopy(d, zz).start()
        v_own(zz).start()

    c_w.wait()

    @pl.when(z + 1 < nz)
    def _():
        w_up_copy(z).start()

    @pl.when(z > 0)
    def _():
        w_down_copy(z).start()

    w_x_copy(0, z).start()
    c_x.wait()

    def x_ycopy(d):
        return remote(
            xf.at[rows_of(mf), :], xf.at[rows_of(mf), :], x_ysend.at[d], x_recv.at[mf],
            me, lax.rem(mf + 2 * d, nf),
        )

    def x_scopy(f):
        return remote(
            xf.at[rows_of(f), :], xf.at[rows_of(f), :], x_ssend.at[f], x_recv.at[f], me, sib
        )

    for d in range(1, ny):
        x_ycopy(d).start()
    x_scopy(mf).start()
    v_start(z)

    @pl.loop(1, n)
    def _(d):
        src = lax.rem(me + d, n)
        id_copy(src, src).wait_recv()

    c_ids = pltpu.make_async_copy(inbox, ids_sm, i_loc.at[0])
    c_ids.start()
    c_kv.wait()
    c_ids.wait()

    def head_slice(h):
        return slice(h * HD, (h + 1) * HD)

    @pl.loop(1, n)
    def _(d):
        peer = lax.rem(me + d, n)
        want = jnp.int32(0)
        for j in range(tiles * topk):
            one = ids_sm[peer, j // topk, j % topk]
            want = jnp.where(one // mb_dev == me, lax.rem(one, mb_dev), want)
        for h in range(heads):
            outbox[peer, h] = kv[want, :, :, head_slice(h)]

    mine = jnp.int32(0)
    for j in range(tiles * topk):
        one = ids_s[j // topk, j % topk]
        mine = jnp.where(one // mb_dev == me, lax.rem(one, mb_dev), mine)
    for h in range(heads):
        ids_in[me, h] = kv[mine, :, :, head_slice(h)]

    def block_copy(peer, slot, h):
        return remote(
            outbox.at[peer, h], ids_in.at[slot, h], m_send.at[peer, h], m_recv.at[slot, h],
            peer, mf,
        )

    def send_blocks(hs, wanted):
        for h in hs:
            @pl.loop(1, n)
            def _(d):
                peer = lax.rem(me + n - d, n)

                @pl.when(wanted(peer // nx, lax.rem(peer, nx)))
                def _():
                    block_copy(peer, me, h).start()

    def inner(pz):
        return (pz > 0) & (pz < nz - 1)

    for k in range(1, nz):
        @pl.when(z - k >= 0)
        def _():
            w_up_copy(z - k).wait_recv()

            @pl.when(z + 1 < nz)
            def _():
                w_up_copy(z - k).start()

            w_x_copy(0, z - k).start()
            v_start(z - k)

        @pl.when(z + k < nz)
        def _():
            w_down_copy(z + k).wait_recv()

            @pl.when(z > 0)
            def _():
                w_down_copy(z + k).start()

            w_x_copy(0, z + k).start()
            v_start(z + k)

        if k == min(2, nz - 1):
            send_blocks(range(heads), lambda pz, px: (px == xx) & inner(pz))
            for d in range(1, ny):
                f = lax.rem(mf + 2 * d, nf)
                x_scopy(f).wait_recv()
                x_scopy(f).start()

    send_blocks(range(heads), lambda pz, px: (px == xx) & jnp.logical_not(inner(pz)))
    send_blocks(range(heads), lambda pz, px: px != xx)

    for d in range(ny):
        x_scopy(lax.rem(sib + 2 * d, nf)).wait_recv()

    q32[...] = jnp.zeros_like(q32)

    def project(slot):
        q32[...] += dot_nn(xf[:, pl.ds(pl.multiple_of(slot * dk, dk), dk)], wf[slot])

    def by_distance(body):
        body(z)
        for k in range(1, nz):
            for zz in (z - k, z + k):
                @pl.when((zz >= 0) & (zz < nz))
                def _():
                    body(zz)

    @pl.loop(0, nz)
    def _(zz):
        project(zz * nx + xx)

    for r in range(nx - 1):
        def arrived(zz):
            w_x_arrival(r, zz).wait_recv()
            if r + 1 < nx - 1:
                w_x_copy(r + 1, zz).start()
            project(zz * nx + lax.rem(xx - 1 - r + 2 * nx, nx))

        by_distance(arrived)

    qb[...] = q32[...].astype(jnp.bfloat16)
    c_lkv.wait()
    c_go.wait()

    scale = 1.0 / math.sqrt(HD)
    rate = scale * math.log2(math.e)
    causal = lax.broadcasted_iota(jnp.int32, (BLK, BLK), 0) >= (
        lax.broadcasted_iota(jnp.int32, (BLK, BLK), 1)
    )

    def attend(h):
        cols = pl.ds(pl.multiple_of(h * HD, HD), HD)

        @pl.loop(1, n)
        def _(d):
            src = lax.rem(me + d, n)
            block_copy(src, src, h).wait_recv()

        stage[...] = ids_in[:, h]
        for t in range(tiles):
            rows = slice(t * BLK, (t + 1) * BLK)
            span = (t + 1) * BLK
            owners = [ids_s[t, j] // mb_dev for j in range(topk)]
            keys = jnp.concatenate(
                [stage[o, 0] for o in owners] + [lkv[0, 0:span, cols]], axis=0
            )
            vals = jnp.concatenate(
                [stage[o, 1] for o in owners] + [lkv[1, 0:span, cols]], axis=0
            )
            s = dot_nt(qb[rows, cols], keys)
            dp = dot_nt(go[rows, cols], vals)
            edge = s.shape[1] - BLK
            s = jnp.concatenate(
                [s[:, :edge], jnp.where(causal, s[:, edge:], NEG_FILL)], axis=1
            )
            top = jnp.max(s, axis=1, keepdims=True)
            e = jnp.exp2((s - top) * rate)
            inv = 1.0 / jnp.sum(e, axis=1, keepdims=True)
            att_ref[rows, cols] = (dot_nn(e.astype(jnp.bfloat16), vals) * inv).astype(
                jnp.bfloat16
            )
            delta = jnp.sum(e * dp, axis=1, keepdims=True) * inv
            ds = (e * (dp - delta)).astype(jnp.bfloat16)
            gq[rows, cols] = (dot_nn(ds, keys) * (inv * scale)).astype(jnp.bfloat16)

    groups = n // per
    near = nz // per

    def slot_of(p):
        return lax.rem(p, nz) * nx + lax.rem(xx + p // nz, nx)

    def span_of(g):
        return pl.ds(g * per, per)

    own_half = pl.ds(pl.multiple_of(cc * rows_dev, rows_dev), rows_dev)
    sib_half = pl.ds(pl.multiple_of((1 - cc) * rows_dev, rows_dev), rows_dev)

    def rs_s(d, g):
        return remote(
            part.at[d, span_of(g), sib_half, :], s_recv.at[d, span_of(g)],
            r_ssend.at[d, g], r_srecv.at[d, g], me, sib,
        )

    def rs_y(d, g):
        return remote(
            y_send.at[d, span_of(g)], y_recv.at[d, span_of(g)],
            r_ysend.at[d, g], r_yrecv.at[d, g], me, lax.rem(mf + 2 * d, nf),
        )

    def shares(first, last, cols):
        for d in list(range(1, ny)) + [0]:
            chip = lax.rem(yy + d, ny)
            rows = pl.ds(pl.multiple_of(chip * 2 * rows_dev, 2 * rows_dev), 2 * rows_dev)

            @pl.loop(first, last)
            def _(g):
                for i in range(per):
                    p = g * per + i
                    part[d, p] = dot_nt(gq[rows, cols], wf[slot_of(p), :, cols]).astype(
                        jnp.bfloat16
                    )
                rs_s(d, g).start()

        for d in range(1, ny):
            @pl.loop(first, last)
            def _(g):
                rs_s(d, g).wait_recv()
                for i in range(per):
                    p = g * per + i
                    y_send[d, p] = (
                        part[d, p, own_half, :].astype(jnp.float32)
                        + s_recv[d, p].astype(jnp.float32)
                    ).astype(jnp.bfloat16)
                rs_y(d, g).start()

    def settled(p):
        total = part[0, p, own_half, :].astype(jnp.float32) + s_recv[0, p].astype(jnp.float32)
        for d in range(1, ny):
            total = total + y_recv[d, p].astype(jnp.float32)
        return total

    def g_copy(f, src):
        return remote(
            gq.at[rows_of(f), late_cols], gq_in.at[src], g_send.at[f], g_recv.at[src], me, f
        )

    @pl.loop(0, early)
    def _(h):
        attend(h)

    shares(0, near, slice(0, late))

    for d in range(1, ny):
        f = lax.rem(mf + 2 * d, nf)

        @pl.loop(0, nz)
        def _(zz):
            v_fwd(f, zz).wait_recv()
            v_fwd(f, zz).start()

    @pl.loop(early, heads)
    def _(h):
        attend(h)

    for d in range(1, nf):
        g_copy(lax.rem(mf + d, nf), mf).start()

    shares(near, groups, slice(0, width))

    for d in range(ny):
        f = lax.rem(sib + 2 * d, nf)

        @pl.loop(0, nz)
        def _(zz):
            v_fwd(f, zz).wait_recv()

    for d in range(1, nf):
        f = lax.rem(mf + d, nf)
        g_copy(f, f).wait_recv()

    def finish(g):
        rs_s(0, g).wait_recv()
        for d in range(1, ny):
            rs_y(d, g).wait_recv()

    def out_cols(p):
        return pl.ds(pl.multiple_of(slot_of(p) * dk, dk), dk)

    @pl.loop(0, near)
    def _(g):
        finish(g)
        for i in range(per):
            p = g * per + i
            total = settled(p) + dot_nt(gq[rows_of(mf), late_cols], wf[slot_of(p), :, late_cols])
            for d in range(1, nf):
                f = lax.rem(mf + d, nf)
                total = total + dot_nt(gq_in[f], wy[f, p])
            gin_ref[:, out_cols(p)] = total.astype(jnp.bfloat16)

    @pl.loop(near, groups)
    def _(g):
        finish(g)
        for i in range(per):
            p = g * per + i
            gin_ref[:, out_cols(p)] = settled(p).astype(jnp.bfloat16)

    @pl.loop(1, n)
    def _(d):
        peer = lax.rem(me + d, n)
        id_copy(peer, me).wait_send()
        for h in range(heads):
            block_copy(peer, me, h).wait_send()

    @pl.loop(0, nz)
    def _(zz):
        @pl.when((zz <= z) & (z + 1 < nz))
        def _():
            w_up_copy(zz).wait_send()

        @pl.when((zz >= z) & (z > 0))
        def _():
            w_down_copy(zz).wait_send()

        for r in range(nx - 1):
            w_x_copy(r, zz).wait_send()
        for d in range(1, ny):
            v_ycopy(d, zz).wait_send()
            v_fwd(lax.rem(mf + 2 * d, nf), zz).wait_send()
        v_own(zz).wait_send()

    for d in range(ny):
        if d:
            x_ycopy(d).wait_send()
        x_scopy(lax.rem(mf + 2 * d, nf)).wait_send()

        @pl.loop(0, groups)
        def _(g):
            rs_s(d, g).wait_send()
            if d:
                rs_y(d, g).wait_send()

    for d in range(1, nf):
        g_copy(lax.rem(mf + d, nf), mf).wait_send()


def emit(a_ref, b_ref, c_ref, d_ref):
    c_ref[...] = a_ref[...]
    d_ref[...] = b_ref[...]


def local(n, nf, layer_input, w_query, local_kv, memory_kv, memory_ids, grad_out):
    nx = 2 ** ((n.bit_length() - 1) // 2)
    nz = n // nx
    ny = nf // 2
    rows_dev, d_model = layer_input.shape
    dk, width = w_query.shape
    ctx = rows_dev * nf
    mb_dev = memory_kv.shape[0]
    bf, f32, i32 = jnp.bfloat16, jnp.float32, jnp.int32
    any_spec = pl.BlockSpec(memory_space=pl.ANY)
    vmem_spec = pl.BlockSpec(memory_space=pltpu.VMEM)
    dma = pltpu.SemaphoreType.DMA
    heads = width // HD
    early = heads // 2
    lw = width - early * HD
    per = max(1, nz // 4)
    groups = n // per
    blocks = pltpu.VMEM((n, heads, 2, BLK, HD), bf)
    piece = pltpu.VMEM((ny, n, rows_dev, dk), bf)
    outs = (
        jax.ShapeDtypeStruct((ctx, width), bf),
        jax.ShapeDtypeStruct((rows_dev, d_model), bf),
    )
    raw = pl.pallas_call(
        functools.partial(kernel, n, nx, nf, mb_dev, early, per),
        out_shape=outs,
        in_specs=[pl.BlockSpec(memory_space=pltpu.SMEM), vmem_spec] + [any_spec] * 5,
        out_specs=(vmem_spec, vmem_spec),
        scratch_shapes=[
            pltpu.VMEM((n, dk, width), bf),
            pltpu.VMEM((ctx, d_model), bf),
            pltpu.VMEM(memory_kv.shape, bf),
            pltpu.VMEM(local_kv.shape, bf),
            pltpu.VMEM(grad_out.shape, bf),
            blocks,
            pltpu.VMEM((n,) + memory_ids.shape, i32),
            pltpu.VMEM((n, 2, BLK, HD), bf),
            blocks,
            pltpu.SMEM((n,) + memory_ids.shape, i32),
            pltpu.VMEM((ctx, width), f32),
            pltpu.VMEM((ctx, width), bf),
            pltpu.VMEM((ctx, width), bf),
            pltpu.VMEM((ny, n, 2 * rows_dev, dk), bf), piece, piece, piece,
            pltpu.VMEM((nf, nz, dk, lw), bf),
            pltpu.VMEM((nf, rows_dev, lw), bf),
            dma((5,)), dma((n,)), dma((n,)), dma((1,)),
            dma((nz,)), dma((nz,)), dma((max(nx - 1, 1), nz)), dma((nz,)),
            dma((max(nx - 1, 1), nz)),
            dma((ny,)), dma((nf,)), dma((nf,)), dma((n, heads)), dma((n, heads)),
            dma((ny, groups)), dma((ny, groups)), dma((ny, groups)), dma((ny, groups)),
            dma((ny, nz)), dma((nf, nz)), dma((nf, nz)), dma((nf,)), dma((nf,)),
        ],
        compiler_params=pltpu.CompilerParams(
            collective_id=0, has_side_effects=True, vmem_limit_bytes=62 * 1024 * 1024
        ),
    )(memory_ids, memory_ids, layer_input, w_query, local_kv, memory_kv, grad_out)
    return pl.pallas_call(emit, out_shape=outs)(*raw)


def solution(mesh):
    placed = (
        P(("mem", "fsdp"), None),
        P("mem", "fsdp"),
        P(None, "mem", "fsdp"),
        P("mem", None, None, "fsdp"),
        P("mem", None),
        P("mem", "fsdp"),
    )
    return jax.shard_map(
        functools.partial(local, mesh.shape["mem"], mesh.shape["fsdp"]),
        mesh=mesh,
        in_specs=placed,
        out_specs=(P("mem", "fsdp"), P(("mem", "fsdp"), None)),
        check_vma=False,
    )
```

```python
import functools
import math

import jax
import jax.numpy as jnp
from jax import lax
from jax.experimental import pallas as pl
from jax.experimental.pallas import tpu as pltpu
from jax.sharding import PartitionSpec as P

HD = 128
BLK = 128
NEG_FILL = -1e30
MESH = pl.DeviceIdType.MESH
NT = (((1,), (1,)), ((), ()))


def dot_nn(a, b):
    return jnp.dot(a, b, preferred_element_type=jnp.float32)


def dot_nt(a, b):
    return lax.dot_general(a, b, NT, preferred_element_type=jnp.float32)


def kernel(
    n, nx, nf, mb_dev, early, per, full, swap,
    ids_s, ids_v, x_hbm, w_hbm, lkv_hbm, mkv_hbm, go_hbm,
    att_ref, gin_ref,
    wf, xf, kv, lkv, go, outbox, inbox, stage, ids_in, ids_sm, q32, qb, gq,
    part, s_recv, y_send, y_recv, wy, gq_in,
    l_sem, i_send, i_recv, i_loc, w_up, w_down, w_x, w_recv, wx_recv,
    x_ysend, x_ssend, x_recv, m_send, m_recv, r_ssend, r_srecv, r_ysend, r_yrecv,
    v_ysend, v_ssend, v_recv, g_send, g_recv,
):
    me = lax.axis_index("mem")
    mf = lax.axis_index("fsdp")
    nz = n // nx
    z, xx = me // nx, lax.rem(me, nx)
    ny = nf // 2
    yy, cc = mf // 2, lax.rem(mf, 2)
    sib = mf + 1 - 2 * cc
    dk = wf.shape[1]
    width = wf.shape[2]
    heads = width // HD
    tiles, topk = ids_s.shape
    rows_dev = xf.shape[0] // nf
    late = early * HD
    late_cols = slice(late, width)
    halves = (slice(0, late), late_cols)

    def local_copy(src, dst, k):
        return pltpu.make_async_copy(src, dst, l_sem.at[k])

    def rows_of(f):
        return pl.ds(pl.multiple_of(f * rows_dev, rows_dev), rows_dev)

    c_w = local_copy(w_hbm, wf.at[me], 0)
    c_x = local_copy(x_hbm, xf.at[rows_of(mf), :], 1)
    c_kv = local_copy(mkv_hbm, kv, 2)
    c_lkv = local_copy(lkv_hbm, lkv, 3)
    c_go = local_copy(go_hbm, go, 4)
    c_w.start()
    c_x.start()
    c_kv.start()
    c_lkv.start()
    c_go.start()

    barrier = pltpu.get_barrier_semaphore()

    @pl.loop(1, n)
    def _(d):
        pl.semaphore_signal(
            barrier, inc=1, device_id=(lax.rem(me + d, n), mf), device_id_type=MESH
        )

    for d in range(1, nf):
        pl.semaphore_signal(
            barrier, inc=1, device_id=(me, lax.rem(mf + d, nf)), device_id_type=MESH
        )
    pl.semaphore_wait(barrier, n - 1 + nf - 1)

    def remote(src, dst, s, r, dm, df):
        return pltpu.make_async_remote_copy(
            src_ref=src, dst_ref=dst, send_sem=s, recv_sem=r,
            device_id=(dm, df), device_id_type=MESH,
        )

    def id_copy(peer, slot):
        return remote(ids_v, inbox.at[slot], i_send.at[peer], i_recv.at[slot], peer, mf)

    @pl.loop(1, n)
    def _(d):
        id_copy(lax.rem(me + d, n), me).start()

    def w_copy(slot, c, sem, dst_m, rsem):
        piece = wf.at[slot, :, halves[c]]
        return remote(piece, piece, sem, rsem, dst_m, mf)

    def w_up_copy(zz, c):
        return w_copy(zz * nx + xx, c, w_up.at[zz, c], me + nx, w_recv.at[zz, c])

    def w_down_copy(zz, c):
        return w_copy(zz * nx + xx, c, w_down.at[zz, c], me - nx, w_recv.at[zz, c])

    x_next = z * nx + lax.rem(xx + 1, nx)

    def w_x_copy(r, zz, c):
        slot = zz * nx + lax.rem(xx - r + nx, nx)
        return w_copy(slot, c, w_x.at[r, zz, c], x_next, wx_recv.at[r, zz, c])

    def w_x_arrival(r, zz, c):
        slot = zz * nx + lax.rem(xx - 1 - r + 2 * nx, nx)
        return w_copy(slot, c, w_x.at[r, zz, c], x_next, wx_recv.at[r, zz, c])

    def slot_of(p):
        return lax.rem(p + z, nz) * nx + lax.rem(xx - p // nz + nx, nx)

    def v_halves(p):
        return (1, 0) if p < full else (1,)

    def v_first(p, c, s, df):
        return remote(
            wf.at[slot_of(p), :, halves[c]], wy.at[mf, p, :, halves[c]],
            s, v_recv.at[mf, p, c], me, df,
        )

    def v_ycopy(d, p, c):
        return v_first(p, c, v_ysend.at[d, p, c], lax.rem(mf + 2 * d, nf))

    def v_own(p, c):
        return v_first(p, c, v_ssend.at[mf, p, c], sib)

    def v_fwd(f, p, c):
        piece = wy.at[f, p, :, halves[c]]
        return remote(piece, piece, v_ssend.at[f, p, c], v_recv.at[f, p, c], me, sib)

    def v_start(p):
        if p < swap:
            for c in v_halves(p):
                for d in range(1, ny):
                    v_ycopy(d, p, c).start()
                v_own(p, c).start()

    c_w.wait()

    for c in range(2):
        @pl.when(z + 1 < nz)
        def _():
            w_up_copy(z, c).start()

        @pl.when(z > 0)
        def _():
            w_down_copy(z, c).start()

        w_x_copy(0, z, c).start()
    c_x.wait()

    def x_ycopy(d):
        return remote(
            xf.at[rows_of(mf), :], xf.at[rows_of(mf), :], x_ysend.at[d], x_recv.at[mf],
            me, lax.rem(mf + 2 * d, nf),
        )

    def x_scopy(f):
        return remote(
            xf.at[rows_of(f), :], xf.at[rows_of(f), :], x_ssend.at[f], x_recv.at[f], me, sib
        )

    for d in range(1, ny):
        x_ycopy(d).start()
    x_scopy(mf).start()
    v_start(0)

    @pl.loop(1, n)
    def _(d):
        src = lax.rem(me + d, n)
        id_copy(src, src).wait_recv()

    c_ids = pltpu.make_async_copy(inbox, ids_sm, i_loc.at[0])
    c_ids.start()
    c_kv.wait()
    c_ids.wait()

    def head_slice(h):
        return slice(h * HD, (h + 1) * HD)

    @pl.loop(1, n)
    def _(d):
        peer = lax.rem(me + d, n)
        want = jnp.int32(0)
        for j in range(tiles * topk):
            one = ids_sm[peer, j // topk, j % topk]
            want = jnp.where(one // mb_dev == me, lax.rem(one, mb_dev), want)
        for h in range(heads):
            outbox[peer, h] = kv[want, :, :, head_slice(h)]

    mine = jnp.int32(0)
    for j in range(tiles * topk):
        one = ids_s[j // topk, j % topk]
        mine = jnp.where(one // mb_dev == me, lax.rem(one, mb_dev), mine)
    for h in range(heads):
        ids_in[me, h] = kv[mine, :, :, head_slice(h)]

    def block_copy(peer, slot, h):
        return remote(
            outbox.at[peer, h], ids_in.at[slot, h], m_send.at[peer, h], m_recv.at[slot, h],
            peer, mf,
        )

    def send_blocks(hs, wanted):
        for h in hs:
            @pl.loop(1, n)
            def _(d):
                peer = lax.rem(me + n - d, n)

                @pl.when(wanted(peer // nx, lax.rem(peer, nx)))
                def _():
                    block_copy(peer, me, h).start()

    def send_crossing(h):
        send_blocks((h,), lambda pz, px: px != xx)

    def inner(pz):
        return (pz > 0) & (pz < nz - 1)

    for k in range(1, nz):
        for c in range(2):
            @pl.when(z - k >= 0)
            def _():
                w_up_copy(z - k, c).wait_recv()

                @pl.when(z + 1 < nz)
                def _():
                    w_up_copy(z - k, c).start()

                w_x_copy(0, z - k, c).start()
                if c:
                    v_start(nz - k)

            @pl.when(z + k < nz)
            def _():
                w_down_copy(z + k, c).wait_recv()

                @pl.when(z > 0)
                def _():
                    w_down_copy(z + k, c).start()

                w_x_copy(0, z + k, c).start()
                if c:
                    v_start(k)

        if k == min(2, nz - 1):
            send_blocks(range(heads), lambda pz, px: (px == xx) & inner(pz))
            for d in range(1, ny):
                f = lax.rem(mf + 2 * d, nf)
                x_scopy(f).wait_recv()
                x_scopy(f).start()


    for d in range(ny):
        x_scopy(lax.rem(sib + 2 * d, nf)).wait_recv()

    q32[...] = jnp.zeros_like(q32)

    def project(slot):
        q32[...] += dot_nn(xf[:, pl.ds(pl.multiple_of(slot * dk, dk), dk)], wf[slot])

    def send_outer():
        send_blocks(range(heads), lambda pz, px: (px == xx) & jnp.logical_not(inner(pz)))

    def by_distance(body, after=None):
        body(z)
        for k in range(1, nz):
            for zz in (z - k, z + k):
                @pl.when((zz >= 0) & (zz < nz))
                def _():
                    body(zz)
            if after and k == 1:
                after()

    @pl.loop(0, nz)
    def _(zz):
        project(zz * nx + xx)

    for r in range(nx - 1):
        def arrived(zz):
            for c in range(2):
                w_x_arrival(r, zz, c).wait_recv()
                if r + 1 < nx - 1:
                    w_x_copy(r + 1, zz, c).start()
            project(zz * nx + lax.rem(xx - 1 - r + 2 * nx, nx))

        by_distance(arrived, send_outer if r == nx - 2 else None)
    if nx == 1:
        send_outer()
    for p in range(nz, swap):
        v_start(p)
    send_crossing(0)
    send_crossing(1)
    qb[...] = q32[...].astype(jnp.bfloat16)
    c_lkv.wait()
    c_go.wait()

    scale = 1.0 / math.sqrt(HD)
    rate = scale * math.log2(math.e)
    causal = lax.broadcasted_iota(jnp.int32, (BLK, BLK), 0) >= (
        lax.broadcasted_iota(jnp.int32, (BLK, BLK), 1)
    )

    def attend(h):
        cols = pl.ds(pl.multiple_of(h * HD, HD), HD)

        @pl.loop(1, n)
        def _(d):
            src = lax.rem(me + d, n)
            block_copy(src, src, h).wait_recv()

        @pl.when(h + 2 < heads)
        def _():
            send_crossing(h + 2)

        stage[...] = ids_in[:, h]
        for t in range(tiles):
            rows = slice(t * BLK, (t + 1) * BLK)
            span = (t + 1) * BLK
            owners = [ids_s[t, j] // mb_dev for j in range(topk)]
            keys = jnp.concatenate(
                [stage[o, 0] for o in owners] + [lkv[0, 0:span, cols]], axis=0
            )
            vals = jnp.concatenate(
                [stage[o, 1] for o in owners] + [lkv[1, 0:span, cols]], axis=0
            )
            s = dot_nt(qb[rows, cols], keys)
            dp = dot_nt(go[rows, cols], vals)
            edge = s.shape[1] - BLK
            s = jnp.concatenate(
                [s[:, :edge], jnp.where(causal, s[:, edge:], NEG_FILL)], axis=1
            )
            top = jnp.max(s, axis=1, keepdims=True)
            e = jnp.exp2((s - top) * rate)
            inv = 1.0 / jnp.sum(e, axis=1, keepdims=True)
            att_ref[rows, cols] = (dot_nn(e.astype(jnp.bfloat16), vals) * inv).astype(
                jnp.bfloat16
            )
            delta = jnp.sum(e * dp, axis=1, keepdims=True) * inv
            ds = (e * (dp - delta)).astype(jnp.bfloat16)
            gq[rows, cols] = (dot_nn(ds, keys) * (inv * scale)).astype(jnp.bfloat16)

    groups = n // per

    def span_of(g):
        return pl.ds(g * per, per)

    own_half = pl.ds(pl.multiple_of(cc * rows_dev, rows_dev), rows_dev)
    sib_half = pl.ds(pl.multiple_of((1 - cc) * rows_dev, rows_dev), rows_dev)

    def rs_s(d, g):
        return remote(
            part.at[d, span_of(g), sib_half, :], s_recv.at[d, span_of(g)],
            r_ssend.at[d, g], r_srecv.at[d, g], me, sib,
        )

    def rs_y(d, g):
        return remote(
            y_send.at[d, span_of(g)], y_recv.at[d, span_of(g)],
            r_ysend.at[d, g], r_yrecv.at[d, g], me, lax.rem(mf + 2 * d, nf),
        )

    def shares(first, last, cols):
        for d in list(range(1, ny)) + [0]:
            chip = lax.rem(yy + d, ny)
            rows = pl.ds(pl.multiple_of(chip * 2 * rows_dev, 2 * rows_dev), 2 * rows_dev)

            @pl.loop(first, last)
            def _(g):
                for i in range(per):
                    p = g * per + i
                    part[d, p] = dot_nt(gq[rows, cols], wf[slot_of(p), :, cols]).astype(
                        jnp.bfloat16
                    )
                rs_s(d, g).start()

        for d in range(1, ny):
            @pl.loop(first, last)
            def _(g):
                rs_s(d, g).wait_recv()
                for i in range(per):
                    p = g * per + i
                    y_send[d, p] = (
                        part[d, p, own_half, :].astype(jnp.float32)
                        + s_recv[d, p].astype(jnp.float32)
                    ).astype(jnp.bfloat16)
                rs_y(d, g).start()

    def settled(p):
        total = part[0, p, own_half, :].astype(jnp.float32) + s_recv[0, p].astype(jnp.float32)
        for d in range(1, ny):
            total = total + y_recv[d, p].astype(jnp.float32)
        return total

    def g_copy(f, src, c):
        return remote(
            gq.at[rows_of(f), halves[c]], gq_in.at[src, :, halves[c]],
            g_send.at[f, c], g_recv.at[src, c], me, f,
        )

    def g_start(c):
        for d in range(1, nf):
            g_copy(lax.rem(mf + d, nf), mf, c).start()

    @pl.loop(0, early)
    def _(h):
        attend(h)

    shares(full // per, swap // per, halves[0])
    g_start(0)

    for p in range(swap):
        for c in v_halves(p):
            for d in range(1, ny):
                f = lax.rem(mf + 2 * d, nf)
                v_fwd(f, p, c).wait_recv()
                v_fwd(f, p, c).start()

    @pl.loop(early, heads)
    def _(h):
        attend(h)

    g_start(1)
    shares(swap // per, groups, slice(0, width))

    for p in range(swap):
        for c in v_halves(p):
            for d in range(ny):
                v_fwd(lax.rem(sib + 2 * d, nf), p, c).wait_recv()

    for d in range(1, nf):
        f = lax.rem(mf + d, nf)
        for c in range(2):
            g_copy(f, f, c).wait_recv()

    def finish(g):
        rs_s(0, g).wait_recv()
        for d in range(1, ny):
            rs_y(d, g).wait_recv()

    def out_cols(p):
        return pl.ds(pl.multiple_of(slot_of(p) * dk, dk), dk)

    def gathered(p, cols):
        total = dot_nt(gq[rows_of(mf), cols], wf[slot_of(p), :, cols])
        for d in range(1, nf):
            f = lax.rem(mf + d, nf)
            total = total + dot_nt(gq_in[f, :, cols], wy[f, p, :, cols])
        return total

    @pl.loop(0, full)
    def _(p):
        gin_ref[:, out_cols(p)] = gathered(p, slice(0, width)).astype(jnp.bfloat16)

    @pl.loop(full // per, swap // per)
    def _(g):
        finish(g)
        for i in range(per):
            p = g * per + i
            gin_ref[:, out_cols(p)] = (settled(p) + gathered(p, late_cols)).astype(jnp.bfloat16)

    @pl.loop(swap // per, groups)
    def _(g):
        finish(g)
        for i in range(per):
            p = g * per + i
            gin_ref[:, out_cols(p)] = settled(p).astype(jnp.bfloat16)

    @pl.loop(1, n)
    def _(d):
        peer = lax.rem(me + d, n)
        id_copy(peer, me).wait_send()
        for h in range(heads):
            block_copy(peer, me, h).wait_send()

    @pl.loop(0, nz)
    def _(zz):
        for c in range(2):
            @pl.when((zz <= z) & (z + 1 < nz))
            def _():
                w_up_copy(zz, c).wait_send()

            @pl.when((zz >= z) & (z > 0))
            def _():
                w_down_copy(zz, c).wait_send()

            for r in range(nx - 1):
                w_x_copy(r, zz, c).wait_send()

    for d in range(ny):
        if d:
            x_ycopy(d).wait_send()
        x_scopy(lax.rem(mf + 2 * d, nf)).wait_send()

        @pl.loop(full // per, groups)
        def _(g):
            rs_s(d, g).wait_send()
            if d:
                rs_y(d, g).wait_send()

    for p in range(swap):
        for c in v_halves(p):
            for d in range(1, ny):
                v_ycopy(d, p, c).wait_send()
                v_fwd(lax.rem(mf + 2 * d, nf), p, c).wait_send()
            v_own(p, c).wait_send()
    for d in range(1, nf):
        for c in range(2):
            g_copy(lax.rem(mf + d, nf), mf, c).wait_send()


def emit(a_ref, b_ref, c_ref, d_ref):
    c_ref[...] = a_ref[...]
    d_ref[...] = b_ref[...]


def local(n, nf, layer_input, w_query, local_kv, memory_kv, memory_ids, grad_out):
    nx = 2 ** ((n.bit_length() - 1) // 2)
    nz = n // nx
    ny = nf // 2
    rows_dev, d_model = layer_input.shape
    dk, width = w_query.shape
    ctx = rows_dev * nf
    mb_dev = memory_kv.shape[0]
    bf, f32, i32 = jnp.bfloat16, jnp.float32, jnp.int32
    any_spec = pl.BlockSpec(memory_space=pl.ANY)
    vmem_spec = pl.BlockSpec(memory_space=pltpu.VMEM)
    dma = pltpu.SemaphoreType.DMA
    heads = width // HD
    early = heads // 2
    per = max(1, nz // 4)
    groups = n // per
    full = nz // 2
    swap = min(nz + per, n)
    blocks = pltpu.VMEM((n, heads, 2, BLK, HD), bf)
    piece = pltpu.VMEM((ny, n, rows_dev, dk), bf)
    outs = (
        jax.ShapeDtypeStruct((ctx, width), bf),
        jax.ShapeDtypeStruct((rows_dev, d_model), bf),
    )
    raw = pl.pallas_call(
        functools.partial(kernel, n, nx, nf, mb_dev, early, per, full, swap),
        out_shape=outs,
        in_specs=[pl.BlockSpec(memory_space=pltpu.SMEM), vmem_spec] + [any_spec] * 5,
        out_specs=(vmem_spec, vmem_spec),
        scratch_shapes=[
            pltpu.VMEM((n, dk, width), bf),
            pltpu.VMEM((ctx, d_model), bf),
            pltpu.VMEM(memory_kv.shape, bf),
            pltpu.VMEM(local_kv.shape, bf),
            pltpu.VMEM(grad_out.shape, bf),
            blocks,
            pltpu.VMEM((n,) + memory_ids.shape, i32),
            pltpu.VMEM((n, 2, BLK, HD), bf),
            blocks,
            pltpu.SMEM((n,) + memory_ids.shape, i32),
            pltpu.VMEM((ctx, width), f32),
            pltpu.VMEM((ctx, width), bf),
            pltpu.VMEM((ctx, width), bf),
            pltpu.VMEM((ny, n, 2 * rows_dev, dk), bf), piece, piece, piece,
            pltpu.VMEM((nf, swap, dk, width), bf),
            pltpu.VMEM((nf, rows_dev, width), bf),
            dma((5,)), dma((n,)), dma((n,)), dma((1,)),
            dma((nz, 2)), dma((nz, 2)), dma((max(nx - 1, 1), nz, 2)), dma((nz, 2)),
            dma((max(nx - 1, 1), nz, 2)),
            dma((ny,)), dma((nf,)), dma((nf,)), dma((n, heads)), dma((n, heads)),
            dma((ny, groups)), dma((ny, groups)), dma((ny, groups)), dma((ny, groups)),
            dma((ny, swap, 2)), dma((nf, swap, 2)), dma((nf, swap, 2)),
            dma((nf, 2)), dma((nf, 2)),
        ],
        compiler_params=pltpu.CompilerParams(
            collective_id=0, has_side_effects=True, vmem_limit_bytes=62 * 1024 * 1024
        ),
    )(memory_ids, memory_ids, layer_input, w_query, local_kv, memory_kv, grad_out)
    return pl.pallas_call(emit, out_shape=outs)(*raw)


def solution(mesh):
    placed = (
        P(("mem", "fsdp"), None),
        P("mem", "fsdp"),
        P(None, "mem", "fsdp"),
        P("mem", None, None, "fsdp"),
        P("mem", None),
        P("mem", "fsdp"),
    )
    return jax.shard_map(
        functools.partial(local, mesh.shape["mem"], mesh.shape["fsdp"]),
        mesh=mesh,
        in_specs=placed,
        out_specs=(P("mem", "fsdp"), P(("mem", "fsdp"), None)),
        check_vma=False,
    )
```

```python
import functools
import math

import jax
import jax.numpy as jnp
from jax import lax
from jax.experimental import pallas as pl
from jax.experimental.pallas import tpu as pltpu
from jax.sharding import PartitionSpec as P

HD = 128
BLK = 128
NEG_FILL = -1e30
MESH = pl.DeviceIdType.MESH
NT = (((1,), (1,)), ((), ()))


def dot_nn(a, b):
    return jnp.dot(a, b, preferred_element_type=jnp.float32)


def dot_nt(a, b):
    return lax.dot_general(a, b, NT, preferred_element_type=jnp.float32)


def kernel(
    n, nx, nf, mb_dev, early, per, swap,
    ids_s, ids_v, x_hbm, w_hbm, lkv_hbm, mkv_hbm, go_hbm,
    att_ref, gin_ref,
    wf, xf, kv, lkv, go, outbox, inbox, stage, ids_in, ids_sm, q32, qb, gq,
    part, s_recv, y_send, y_recv, wy, gq_in,
    l_sem, i_send, i_recv, i_loc, w_up, w_down, w_x, w_recv, wx_recv,
    x_ysend, x_ssend, x_recv, m_send, m_recv, r_ssend, r_srecv, r_ysend, r_yrecv,
    v_ysend, v_ssend, v_recv, g_send, g_recv, seen,
):
    me = lax.axis_index("mem")
    mf = lax.axis_index("fsdp")
    nz = n // nx
    z, xx = me // nx, lax.rem(me, nx)
    ny = nf // 2
    yy, cc = mf // 2, lax.rem(mf, 2)
    sib = mf + 1 - 2 * cc
    dk = wf.shape[1]
    width = wf.shape[2]
    heads = width // HD
    tiles, topk = ids_s.shape
    rows_dev = xf.shape[0] // nf
    late = early * HD
    late_cols = slice(late, width)
    halves = (slice(0, late), late_cols)

    def local_copy(src, dst, k):
        return pltpu.make_async_copy(src, dst, l_sem.at[k])

    def rows_of(f):
        return pl.ds(pl.multiple_of(f * rows_dev, rows_dev), rows_dev)

    c_w = local_copy(w_hbm, wf.at[me], 0)
    c_x = local_copy(x_hbm, xf.at[rows_of(mf), :], 1)
    c_kv = local_copy(mkv_hbm, kv, 2)
    c_lkv = local_copy(lkv_hbm, lkv, 3)
    c_go = local_copy(go_hbm, go, 4)
    c_w.start()
    c_x.start()
    c_kv.start()
    c_lkv.start()
    c_go.start()

    barrier = pltpu.get_barrier_semaphore()

    x_next = z * nx + lax.rem(xx + 1, nx)
    x_prev = z * nx + lax.rem(xx + nx - 1, nx)
    below, above = z > 0, z + 1 < nz

    def signal(sem, dm, df):
        pl.semaphore_signal(sem, inc=1, device_id=(dm, df), device_id_type=MESH)

    @pl.when(above)
    def _():
        signal(barrier, me + nx, mf)

    @pl.when(below)
    def _():
        signal(barrier, me - nx, mf)

    signal(barrier, x_next, mf)
    if nx > 2:
        signal(barrier, x_prev, mf)
    for d in range(1, nf):
        signal(barrier, me, lax.rem(mf + d, nf))
    line = (z + nz - 2) // (nz - 1) + (2 * nz - 3 - z) // (nz - 1)
    pl.semaphore_wait(barrier, (1 if nx == 2 else 2) + nf - 1 + line)

    def remote(src, dst, s, r, dm, df):
        return pltpu.make_async_remote_copy(
            src_ref=src, dst_ref=dst, send_sem=s, recv_sem=r,
            device_id=(dm, df), device_id_type=MESH,
        )

    def id_copy(peer, slot):
        return remote(ids_v, inbox.at[slot], i_send.at[peer], i_recv.at[slot], peer, mf)

    def w_copy(slot, c, sem, dst_m, rsem):
        piece = wf.at[slot, :, halves[c]]
        return remote(piece, piece, sem, rsem, dst_m, mf)

    def w_up_copy(zz, c):
        return w_copy(zz * nx + xx, c, w_up.at[zz, c], me + nx, w_recv.at[zz, c])

    def w_down_copy(zz, c):
        return w_copy(zz * nx + xx, c, w_down.at[zz, c], me - nx, w_recv.at[zz, c])

    def w_x_copy(r, zz, c):
        slot = zz * nx + lax.rem(xx - r + nx, nx)
        return w_copy(slot, c, w_x.at[r, zz, c], x_next, wx_recv.at[r, zz, c])

    def w_x_arrival(r, zz, c):
        slot = zz * nx + lax.rem(xx - 1 - r + 2 * nx, nx)
        return w_copy(slot, c, w_x.at[r, zz, c], x_next, wx_recv.at[r, zz, c])

    turn = 1 - 2 * ((z + 1) // nz)

    def slot_of(p):
        return lax.rem(z + turn * lax.rem(p, nz) + nz, nz) * nx + lax.rem(xx - p // nz + nx, nx)

    def v_first(p, s, df):
        return remote(
            wf.at[slot_of(p), :, late_cols], wy.at[mf, p], s, v_recv.at[mf, p], me, df
        )

    def v_ycopy(d, p):
        return v_first(p, v_ysend.at[d, p], lax.rem(mf + 2 * d, nf))

    def v_own(p):
        return v_first(p, v_ssend.at[mf, p], sib)

    def v_fwd(f, p):
        return remote(
            wy.at[f, p], wy.at[f, p], v_ssend.at[f, p], v_recv.at[f, p], me, sib
        )

    def v_start(p):
        for d in range(1, ny):
            v_ycopy(d, p).start()
        v_own(p).start()

    c_w.wait()

    def w_begin(c):
        @pl.when(above)
        def _():
            w_up_copy(z, c).start()

        @pl.when(below)
        def _():
            w_down_copy(z, c).start()

        w_x_copy(0, z, c).start()

    w_begin(0)

    @pl.when(below)
    def _():
        pl.semaphore_wait(seen.at[0], 1)

    @pl.when(above)
    def _():
        signal(seen.at[0], me + nx, mf)
        pl.semaphore_wait(seen.at[1], 1)

    @pl.when(below)
    def _():
        signal(seen.at[1], me - nx, mf)

    for r in range(nx - 1):
        signal(seen.at[2], x_next, mf)
        pl.semaphore_wait(seen.at[2], 1)

    @pl.loop(1, n)
    def _(d):
        id_copy(lax.rem(me + d, n), me).start()

    w_begin(1)
    c_x.wait()

    def x_ycopy(d):
        return remote(
            xf.at[rows_of(mf), :], xf.at[rows_of(mf), :], x_ysend.at[d], x_recv.at[mf],
            me, lax.rem(mf + 2 * d, nf),
        )

    def x_scopy(f):
        return remote(
            xf.at[rows_of(f), :], xf.at[rows_of(f), :], x_ssend.at[f], x_recv.at[f], me, sib
        )

    for d in range(1, ny):
        x_ycopy(d).start()
    x_scopy(mf).start()
    v_start(0)

    def head_slice(h):
        return slice(h * HD, (h + 1) * HD)

    def fill():
        @pl.loop(1, n)
        def _(d):
            src = lax.rem(me + d, n)
            id_copy(src, src).wait_recv()

        c_ids = pltpu.make_async_copy(inbox, ids_sm, i_loc.at[0])
        c_ids.start()
        c_kv.wait()
        c_ids.wait()

        @pl.loop(1, n)
        def _(d):
            peer = lax.rem(me + d, n)
            want = jnp.int32(0)
            for j in range(tiles * topk):
                one = ids_sm[peer, j // topk, j % topk]
                want = jnp.where(one // mb_dev == me, lax.rem(one, mb_dev), want)
            for h in range(heads):
                outbox[peer, h] = kv[want, :, :, head_slice(h)]

        mine = jnp.int32(0)
        for j in range(tiles * topk):
            one = ids_s[j // topk, j % topk]
            mine = jnp.where(one // mb_dev == me, lax.rem(one, mb_dev), mine)
        for h in range(heads):
            ids_in[me, h] = kv[mine, :, :, head_slice(h)]

    def block_copy(peer, slot, h):
        return remote(
            outbox.at[peer, h], ids_in.at[slot, h], m_send.at[peer, h], m_recv.at[slot, h],
            peer, mf,
        )

    def send_blocks(hs, wanted):
        for h in hs:
            @pl.loop(1, n)
            def _(d):
                peer = lax.rem(me + n - d, n)

                @pl.when(wanted(peer // nx, lax.rem(peer, nx)))
                def _():
                    block_copy(peer, me, h).start()

    def send_crossing(h):
        send_blocks((h,), lambda pz, px: px != xx)

    def inner(pz):
        return (pz > 0) & (pz < nz - 1)

    for k in range(1, nz):
        for c in range(2):
            @pl.when(z - k >= 0)
            def _():
                w_up_copy(z - k, c).wait_recv()

                @pl.when(z + 1 < nz)
                def _():
                    w_up_copy(z - k, c).start()

                if c:
                    v_start(nz - k + (2 * k - nz) * ((z + 1) // nz))
                if c == 0 or k < 2:
                    w_x_copy(0, z - k, c).start()

            @pl.when(z + k < nz)
            def _():
                w_down_copy(z + k, c).wait_recv()

                @pl.when(z > 0)
                def _():
                    w_down_copy(z + k, c).start()

                if c:
                    v_start(k)
                if c == 0 or k < 2:
                    w_x_copy(0, z + k, c).start()

        if k == 1:
            fill()
        if k == min(2, nz - 1):
            send_blocks(range(heads), lambda pz, px: (px == xx) & inner(pz))
            for d in range(1, ny):
                f = lax.rem(mf + 2 * d, nf)
                x_scopy(f).wait_recv()
                x_scopy(f).start()


    for d in range(ny):
        x_scopy(lax.rem(sib + 2 * d, nf)).wait_recv()

    q32[...] = jnp.zeros_like(q32)

    def project(slot, c):
        q32[:, halves[c]] += dot_nn(
            xf[:, pl.ds(pl.multiple_of(slot * dk, dk), dk)], wf[slot, :, halves[c]]
        )

    def at_distance(k, body):
        for zz in (z - k, z + k) if k else (z,):
            @pl.when((zz >= 0) & (zz < nz))
            def _():
                body(zz)

    def arrived(r, c):
        def body(zz):
            w_x_arrival(r, zz, c).wait_recv()
            if r + 1 < nx - 1:
                w_x_copy(r + 1, zz, c).start()
            project(zz * nx + lax.rem(xx - 1 - r + 2 * nx, nx), c)

        return body

    def own_column(c):
        @pl.loop(0, nz)
        def _(zz):
            project(zz * nx + xx, c)

    def send_outer(hs):
        send_blocks(hs, lambda pz, px: (px == xx) & jnp.logical_not(inner(pz)))

    own_column(0)
    for r in range(nx - 1):
        for k in range(nz):
            at_distance(k, arrived(r, 0))
            if r == nx - 2 and k == 1:
                send_outer(range(early))
    for h in range(early):
        send_crossing(h)
    for k in range(2, nz):
        at_distance(k, lambda zz: w_x_copy(0, zz, 1).start())
    send_outer(range(early, heads))
    qb[:, halves[0]] = q32[:, halves[0]].astype(jnp.bfloat16)

    own_column(1)
    for k in range(min(2, nz)):
        at_distance(k, arrived(0, 1))
    for p in range(nz, swap):
        v_start(p)
    c_lkv.wait()
    c_go.wait()

    scale = 1.0 / math.sqrt(HD)
    rate = scale * math.log2(math.e)
    causal = lax.broadcasted_iota(jnp.int32, (BLK, BLK), 0) >= (
        lax.broadcasted_iota(jnp.int32, (BLK, BLK), 1)
    )

    def attend(h, then=None):
        cols = pl.ds(pl.multiple_of(h * HD, HD), HD)

        @pl.loop(1, n)
        def _(d):
            src = lax.rem(me + d, n)
            block_copy(src, src, h).wait_recv()

        if then:
            then(h)
        stage[...] = ids_in[:, h]
        for t in range(tiles):
            rows = slice(t * BLK, (t + 1) * BLK)
            span = (t + 1) * BLK
            owners = [ids_s[t, j] // mb_dev for j in range(topk)]
            keys = jnp.concatenate(
                [stage[o, 0] for o in owners] + [lkv[0, 0:span, cols]], axis=0
            )
            vals = jnp.concatenate(
                [stage[o, 1] for o in owners] + [lkv[1, 0:span, cols]], axis=0
            )
            s = dot_nt(qb[rows, cols], keys)
            dp = dot_nt(go[rows, cols], vals)
            edge = s.shape[1] - BLK
            s = jnp.concatenate(
                [s[:, :edge], jnp.where(causal, s[:, edge:], NEG_FILL)], axis=1
            )
            top = jnp.max(s, axis=1, keepdims=True)
            e = jnp.exp2((s - top) * rate)
            inv = 1.0 / jnp.sum(e, axis=1, keepdims=True)
            att_ref[rows, cols] = (dot_nn(e.astype(jnp.bfloat16), vals) * inv).astype(
                jnp.bfloat16
            )
            delta = jnp.sum(e * dp, axis=1, keepdims=True) * inv
            ds = (e * (dp - delta)).astype(jnp.bfloat16)
            gq[rows, cols] = (dot_nn(ds, keys) * (inv * scale)).astype(jnp.bfloat16)

    groups = n // per

    def span_of(g):
        return pl.ds(g * per, per)

    own_half = pl.ds(pl.multiple_of(cc * rows_dev, rows_dev), rows_dev)
    sib_half = pl.ds(pl.multiple_of((1 - cc) * rows_dev, rows_dev), rows_dev)

    def rs_s(d, g):
        return remote(
            part.at[d, span_of(g), sib_half, :], s_recv.at[d, span_of(g)],
            r_ssend.at[d, g], r_srecv.at[d, g], me, sib,
        )

    def rs_y(d, g):
        return remote(
            y_send.at[d, span_of(g)], y_recv.at[d, span_of(g)],
            r_ysend.at[d, g], r_yrecv.at[d, g], me, lax.rem(mf + 2 * d, nf),
        )

    def shares(first, last, cols):
        for d in list(range(1, ny)) + [0]:
            chip = lax.rem(yy + d, ny)
            rows = pl.ds(pl.multiple_of(chip * 2 * rows_dev, 2 * rows_dev), 2 * rows_dev)

            @pl.loop(first, last)
            def _(g):
                for i in range(per):
                    p = g * per + i
                    part[d, p] = dot_nt(gq[rows, cols], wf[slot_of(p), :, cols]).astype(
                        jnp.bfloat16
                    )
                rs_s(d, g).start()

        for d in range(1, ny):
            @pl.loop(first, last)
            def _(g):
                rs_s(d, g).wait_recv()
                for i in range(per):
                    p = g * per + i
                    y_send[d, p] = (
                        part[d, p, own_half, :].astype(jnp.float32)
                        + s_recv[d, p].astype(jnp.float32)
                    ).astype(jnp.bfloat16)
                rs_y(d, g).start()

    def settled(p):
        total = part[0, p, own_half, :].astype(jnp.float32) + s_recv[0, p].astype(jnp.float32)
        for d in range(1, ny):
            total = total + y_recv[d, p].astype(jnp.float32)
        return total

    def g_copy(f, src):
        return remote(
            gq.at[rows_of(f), late_cols], gq_in.at[src], g_send.at[f], g_recv.at[src], me, f
        )

    def resume(h):
        @pl.when(h == early - 1)
        def _():
            for late_head in range(early, heads):
                send_crossing(late_head)

    @pl.loop(0, early)
    def _(h):
        attend(h, resume)

    shares(0, swap // per, halves[0])

    for k in range(2, nz):
        at_distance(k, arrived(0, 1))
    for r in range(1, nx - 1):
        for k in range(nz):
            at_distance(k, arrived(r, 1))
    qb[:, late_cols] = q32[:, late_cols].astype(jnp.bfloat16)

    for d in range(1, ny):
        f = lax.rem(mf + 2 * d, nf)

        @pl.loop(0, swap)
        def _(p):
            v_fwd(f, p).wait_recv()
            v_fwd(f, p).start()

    @pl.loop(early, heads)
    def _(h):
        attend(h)

    for d in range(1, nf):
        g_copy(lax.rem(mf + d, nf), mf).start()

    shares(swap // per, groups, slice(0, width))

    for d in range(ny):
        f = lax.rem(sib + 2 * d, nf)

        @pl.loop(0, swap)
        def _(p):
            v_fwd(f, p).wait_recv()

    for d in range(1, nf):
        f = lax.rem(mf + d, nf)
        g_copy(f, f).wait_recv()

    def finish(g):
        rs_s(0, g).wait_recv()
        for d in range(1, ny):
            rs_y(d, g).wait_recv()

    def out_cols(p):
        return pl.ds(pl.multiple_of(slot_of(p) * dk, dk), dk)

    def gathered(p):
        total = dot_nt(gq[rows_of(mf), late_cols], wf[slot_of(p), :, late_cols])
        for d in range(1, nf):
            f = lax.rem(mf + d, nf)
            total = total + dot_nt(gq_in[f], wy[f, p])
        return total

    @pl.loop(0, swap // per)
    def _(g):
        finish(g)
        for i in range(per):
            p = g * per + i
            gin_ref[:, out_cols(p)] = (settled(p) + gathered(p)).astype(jnp.bfloat16)

    @pl.loop(swap // per, groups)
    def _(g):
        finish(g)
        for i in range(per):
            p = g * per + i
            gin_ref[:, out_cols(p)] = settled(p).astype(jnp.bfloat16)

    @pl.loop(1, n)
    def _(d):
        peer = lax.rem(me + d, n)
        id_copy(peer, me).wait_send()
        for h in range(heads):
            block_copy(peer, me, h).wait_send()

    @pl.loop(0, nz)
    def _(zz):
        for c in range(2):
            @pl.when((zz <= z) & (z + 1 < nz))
            def _():
                w_up_copy(zz, c).wait_send()

            @pl.when((zz >= z) & (z > 0))
            def _():
                w_down_copy(zz, c).wait_send()

            for r in range(nx - 1):
                w_x_copy(r, zz, c).wait_send()

    for d in range(ny):
        if d:
            x_ycopy(d).wait_send()
        x_scopy(lax.rem(mf + 2 * d, nf)).wait_send()

        @pl.loop(0, groups)
        def _(g):
            rs_s(d, g).wait_send()
            if d:
                rs_y(d, g).wait_send()

    @pl.loop(0, swap)
    def _(p):
        for d in range(1, ny):
            v_ycopy(d, p).wait_send()
            v_fwd(lax.rem(mf + 2 * d, nf), p).wait_send()
        v_own(p).wait_send()

    for d in range(1, nf):
        g_copy(lax.rem(mf + d, nf), mf).wait_send()


def emit(a_ref, b_ref, c_ref, d_ref):
    c_ref[...] = a_ref[...]
    d_ref[...] = b_ref[...]


def local(n, nf, layer_input, w_query, local_kv, memory_kv, memory_ids, grad_out):
    nx = 2 ** ((n.bit_length() - 1) // 2)
    nz = n // nx
    ny = nf // 2
    rows_dev, d_model = layer_input.shape
    dk, width = w_query.shape
    ctx = rows_dev * nf
    mb_dev = memory_kv.shape[0]
    bf, f32, i32 = jnp.bfloat16, jnp.float32, jnp.int32
    any_spec = pl.BlockSpec(memory_space=pl.ANY)
    vmem_spec = pl.BlockSpec(memory_space=pltpu.VMEM)
    dma = pltpu.SemaphoreType.DMA
    heads = width // HD
    early = heads // 2
    per = max(1, nz // 4)
    groups = n // per
    lw = width - early * HD
    swap = min(nz + 2, n)
    blocks = pltpu.VMEM((n, heads, 2, BLK, HD), bf)
    piece = pltpu.VMEM((ny, n, rows_dev, dk), bf)
    outs = (
        jax.ShapeDtypeStruct((ctx, width), bf),
        jax.ShapeDtypeStruct((rows_dev, d_model), bf),
    )
    raw = pl.pallas_call(
        functools.partial(kernel, n, nx, nf, mb_dev, early, per, swap),
        out_shape=outs,
        in_specs=[pl.BlockSpec(memory_space=pltpu.SMEM), vmem_spec] + [any_spec] * 5,
        out_specs=(vmem_spec, vmem_spec),
        scratch_shapes=[
            pltpu.VMEM((n, dk, width), bf),
            pltpu.VMEM((ctx, d_model), bf),
            pltpu.VMEM(memory_kv.shape, bf),
            pltpu.VMEM(local_kv.shape, bf),
            pltpu.VMEM(grad_out.shape, bf),
            blocks,
            pltpu.VMEM((n,) + memory_ids.shape, i32),
            pltpu.VMEM((n, 2, BLK, HD), bf),
            blocks,
            pltpu.SMEM((n,) + memory_ids.shape, i32),
            pltpu.VMEM((ctx, width), f32),
            pltpu.VMEM((ctx, width), bf),
            pltpu.VMEM((ctx, width), bf),
            pltpu.VMEM((ny, n, 2 * rows_dev, dk), bf), piece, piece, piece,
            pltpu.VMEM((nf, swap, dk, lw), bf),
            pltpu.VMEM((nf, rows_dev, lw), bf),
            dma((5,)), dma((n,)), dma((n,)), dma((1,)),
            dma((nz, 2)), dma((nz, 2)), dma((max(nx - 1, 1), nz, 2)), dma((nz, 2)),
            dma((max(nx - 1, 1), nz, 2)),
            dma((ny,)), dma((nf,)), dma((nf,)), dma((n, heads)), dma((n, heads)),
            dma((ny, groups)), dma((ny, groups)), dma((ny, groups)), dma((ny, groups)),
            dma((ny, swap)), dma((nf, swap)), dma((nf, swap)),
            dma((nf,)), dma((nf,)), pltpu.SemaphoreType.REGULAR((3,)),
        ],
        compiler_params=pltpu.CompilerParams(
            collective_id=0, has_side_effects=True, vmem_limit_bytes=62 * 1024 * 1024
        ),
    )(memory_ids, memory_ids, layer_input, w_query, local_kv, memory_kv, grad_out)
    return pl.pallas_call(emit, out_shape=outs)(*raw)


def solution(mesh):
    placed = (
        P(("mem", "fsdp"), None),
        P("mem", "fsdp"),
        P(None, "mem", "fsdp"),
        P("mem", None, None, "fsdp"),
        P("mem", None),
        P("mem", "fsdp"),
    )
    return jax.shard_map(
        functools.partial(local, mesh.shape["mem"], mesh.shape["fsdp"]),
        mesh=mesh,
        in_specs=placed,
        out_specs=(P("mem", "fsdp"), P(("mem", "fsdp"), None)),
        check_vma=False,
    )
```

```python
import functools
import math

import jax
import jax.numpy as jnp
from jax import lax
from jax.experimental import pallas as pl
from jax.experimental.pallas import tpu as pltpu
from jax.sharding import PartitionSpec as P

HD = 128
BLK = 128
NEG_FILL = -1e30
LAG = 3
MESH = pl.DeviceIdType.MESH
NT = (((1,), (1,)), ((), ()))


def dot_nn(a, b):
    return jnp.dot(a, b, preferred_element_type=jnp.float32)


def dot_nt(a, b):
    return lax.dot_general(a, b, NT, preferred_element_type=jnp.float32)


def kernel(
    n, nx, nf, mb_dev, early, per, swap,
    ids_s, ids_v, x_hbm, w_hbm, lkv_hbm, mkv_hbm, go_hbm,
    att_hbm, gin_hbm,
    wf, xf, kv, lkv, go, outbox, inbox, stage, ids_in, ids_sm, q32, qb, gq,
    part, s_recv, y_send, y_recv, wy, gq_in,
    l_sem, i_send, i_recv, i_loc, w_up, w_down, w_x, w_recv, wx_recv,
    x_ysend, x_ssend, x_recv, m_send, m_recv, r_ssend, r_srecv, r_ysend, r_yrecv,
    v_ysend, v_ssend, v_recv, g_send, g_recv, seen, att_ref, gin_ref, o_sem,
):
    me = lax.axis_index("mem")
    mf = lax.axis_index("fsdp")
    nz = n // nx
    z, xx = me // nx, lax.rem(me, nx)
    ny = nf // 2
    yy, cc = mf // 2, lax.rem(mf, 2)
    sib = mf + 1 - 2 * cc
    dk = wf.shape[1]
    width = wf.shape[2]
    heads = width // HD
    tiles, topk = ids_s.shape
    rows_dev = xf.shape[0] // nf
    late = early * HD
    late_cols = slice(late, width)
    halves = (slice(0, late), late_cols)

    def local_copy(src, dst, k):
        return pltpu.make_async_copy(src, dst, l_sem.at[k])

    def rows_of(f):
        return pl.ds(pl.multiple_of(f * rows_dev, rows_dev), rows_dev)

    c_w = local_copy(w_hbm, wf.at[me], 0)
    c_x = local_copy(x_hbm, xf.at[rows_of(mf), :], 1)
    c_kv = local_copy(mkv_hbm, kv, 2)
    c_lkv = local_copy(lkv_hbm, lkv, 3)
    c_go = local_copy(go_hbm, go, 4)
    c_w.start()
    c_x.start()
    c_kv.start()
    c_lkv.start()
    c_go.start()

    barrier = pltpu.get_barrier_semaphore()

    x_next = z * nx + lax.rem(xx + 1, nx)
    x_prev = z * nx + lax.rem(xx + nx - 1, nx)
    below, above = z > 0, z + 1 < nz

    def signal(sem, dm, df):
        pl.semaphore_signal(sem, inc=1, device_id=(dm, df), device_id_type=MESH)

    @pl.when(above)
    def _():
        signal(barrier, me + nx, mf)

    @pl.when(below)
    def _():
        signal(barrier, me - nx, mf)

    signal(barrier, x_next, mf)
    if nx > 2:
        signal(barrier, x_prev, mf)
    for d in range(1, nf):
        signal(barrier, me, lax.rem(mf + d, nf))
    line = (z + nz - 2) // (nz - 1) + (2 * nz - 3 - z) // (nz - 1)
    pl.semaphore_wait(barrier, (1 if nx == 2 else 2) + nf - 1 + line)

    def remote(src, dst, s, r, dm, df):
        return pltpu.make_async_remote_copy(
            src_ref=src, dst_ref=dst, send_sem=s, recv_sem=r,
            device_id=(dm, df), device_id_type=MESH,
        )

    def id_copy(peer, slot):
        return remote(ids_v, inbox.at[slot], i_send.at[peer], i_recv.at[slot], peer, mf)

    def w_copy(slot, c, sem, dst_m, rsem):
        piece = wf.at[slot, :, halves[c]]
        return remote(piece, piece, sem, rsem, dst_m, mf)

    def w_up_copy(zz, c):
        return w_copy(zz * nx + xx, c, w_up.at[zz, c], me + nx, w_recv.at[zz, c])

    def w_down_copy(zz, c):
        return w_copy(zz * nx + xx, c, w_down.at[zz, c], me - nx, w_recv.at[zz, c])

    def w_x_copy(r, zz, c):
        slot = zz * nx + lax.rem(xx - r + nx, nx)
        return w_copy(slot, c, w_x.at[r, zz, c], x_next, wx_recv.at[r, zz, c])

    def w_x_arrival(r, zz, c):
        slot = zz * nx + lax.rem(xx - 1 - r + 2 * nx, nx)
        return w_copy(slot, c, w_x.at[r, zz, c], x_next, wx_recv.at[r, zz, c])

    turn = 1 - 2 * ((z + 1) // nz)

    def slot_of(p):
        return lax.rem(z + turn * lax.rem(p, nz) + nz, nz) * nx + lax.rem(xx - p // nz + nx, nx)

    def v_first(p, s, df):
        return remote(
            wf.at[slot_of(p), :, late_cols], wy.at[mf, p], s, v_recv.at[mf, p], me, df
        )

    def v_ycopy(d, p):
        return v_first(p, v_ysend.at[d, p], lax.rem(mf + 2 * d, nf))

    def v_own(p):
        return v_first(p, v_ssend.at[mf, p], sib)

    def v_fwd(f, p):
        return remote(
            wy.at[f, p], wy.at[f, p], v_ssend.at[f, p], v_recv.at[f, p], me, sib
        )

    def v_start(p):
        for d in range(1, ny):
            v_ycopy(d, p).start()
        v_own(p).start()

    c_w.wait()

    def w_begin(c):
        @pl.when(above)
        def _():
            w_up_copy(z, c).start()

        @pl.when(below)
        def _():
            w_down_copy(z, c).start()

        w_x_copy(0, z, c).start()

    w_begin(0)

    @pl.when(below)
    def _():
        pl.semaphore_wait(seen.at[0], 1)

    @pl.when(above)
    def _():
        signal(seen.at[0], me + nx, mf)
        pl.semaphore_wait(seen.at[1], 1)

    @pl.when(below)
    def _():
        signal(seen.at[1], me - nx, mf)

    for r in range(nx - 1):
        signal(seen.at[2], x_next, mf)
        pl.semaphore_wait(seen.at[2], 1)

    @pl.loop(1, n)
    def _(d):
        id_copy(lax.rem(me + d, n), me).start()

    w_begin(1)
    c_x.wait()

    def x_ycopy(d):
        return remote(
            xf.at[rows_of(mf), :], xf.at[rows_of(mf), :], x_ysend.at[d], x_recv.at[mf],
            me, lax.rem(mf + 2 * d, nf),
        )

    def x_scopy(f):
        return remote(
            xf.at[rows_of(f), :], xf.at[rows_of(f), :], x_ssend.at[f], x_recv.at[f], me, sib
        )

    for d in range(1, ny):
        x_ycopy(d).start()
    x_scopy(mf).start()
    v_start(0)

    def head_slice(h):
        return slice(h * HD, (h + 1) * HD)

    def fill():
        @pl.loop(1, n)
        def _(d):
            src = lax.rem(me + d, n)
            id_copy(src, src).wait_recv()

        c_ids = pltpu.make_async_copy(inbox, ids_sm, i_loc.at[0])
        c_ids.start()
        c_kv.wait()
        c_ids.wait()

        @pl.loop(1, n)
        def _(d):
            peer = lax.rem(me + d, n)
            want = jnp.int32(0)
            for j in range(tiles * topk):
                one = ids_sm[peer, j // topk, j % topk]
                want = jnp.where(one // mb_dev == me, lax.rem(one, mb_dev), want)
            for h in range(heads):
                outbox[peer, h] = kv[want, :, :, head_slice(h)]

        mine = jnp.int32(0)
        for j in range(tiles * topk):
            one = ids_s[j // topk, j % topk]
            mine = jnp.where(one // mb_dev == me, lax.rem(one, mb_dev), mine)
        for h in range(heads):
            ids_in[me, h] = kv[mine, :, :, head_slice(h)]

    def block_copy(peer, slot, h):
        return remote(
            outbox.at[peer, h], ids_in.at[slot, h], m_send.at[peer, h], m_recv.at[slot, h],
            peer, mf,
        )

    def send_blocks(hs, wanted):
        for h in hs:
            @pl.loop(1, n)
            def _(d):
                peer = lax.rem(me + n - d, n)

                @pl.when(wanted(peer // nx, lax.rem(peer, nx)))
                def _():
                    block_copy(peer, me, h).start()

    def send_crossing(h):
        send_blocks((h,), lambda pz, px: px != xx)

    def inner(pz):
        return (pz > 0) & (pz < nz - 1)

    for k in range(1, nz):
        for c in range(2):
            @pl.when(z - k >= 0)
            def _():
                w_up_copy(z - k, c).wait_recv()

                @pl.when(z + 1 < nz)
                def _():
                    w_up_copy(z - k, c).start()

                if c:
                    v_start(nz - k + (2 * k - nz) * ((z + 1) // nz))
                if c == 0 or k < 2:
                    w_x_copy(0, z - k, c).start()

            @pl.when(z + k < nz)
            def _():
                w_down_copy(z + k, c).wait_recv()

                @pl.when(z > 0)
                def _():
                    w_down_copy(z + k, c).start()

                if c:
                    v_start(k)
                if c == 0 or k < 2:
                    w_x_copy(0, z + k, c).start()

        if k == 1:
            fill()
        if k == min(2, nz - 1):
            send_blocks(range(heads), lambda pz, px: (px == xx) & inner(pz))
            for d in range(1, ny):
                f = lax.rem(mf + 2 * d, nf)
                x_scopy(f).wait_recv()
                x_scopy(f).start()


    for d in range(ny):
        x_scopy(lax.rem(sib + 2 * d, nf)).wait_recv()

    q32[...] = jnp.zeros_like(q32)

    def project(slot, c):
        q32[:, halves[c]] += dot_nn(
            xf[:, pl.ds(pl.multiple_of(slot * dk, dk), dk)], wf[slot, :, halves[c]]
        )

    def at_distance(k, body):
        for zz in (z - k, z + k) if k else (z,):
            @pl.when((zz >= 0) & (zz < nz))
            def _():
                body(zz)

    def arrived(r, c):
        def body(zz):
            w_x_arrival(r, zz, c).wait_recv()
            if r + 1 < nx - 1:
                w_x_copy(r + 1, zz, c).start()
            project(zz * nx + lax.rem(xx - 1 - r + 2 * nx, nx), c)

        return body

    def own_column(c):
        @pl.loop(0, nz)
        def _(zz):
            project(zz * nx + xx, c)

    def send_outer(hs):
        send_blocks(hs, lambda pz, px: (px == xx) & jnp.logical_not(inner(pz)))

    own_column(0)
    for r in range(nx - 1):
        for k in range(nz):
            at_distance(k, arrived(r, 0))
            if r == nx - 2 and k == 1:
                send_outer(range(early))
    for h in range(early):
        send_crossing(h)
    for k in range(2, nz):
        at_distance(k, lambda zz: w_x_copy(0, zz, 1).start())
    send_outer(range(early, heads))
    qb[:, halves[0]] = q32[:, halves[0]].astype(jnp.bfloat16)

    own_column(1)
    for k in range(min(2, nz)):
        at_distance(k, arrived(0, 1))
    for p in range(nz, swap):
        v_start(p)
    c_lkv.wait()
    c_go.wait()

    scale = 1.0 / math.sqrt(HD)
    rate = scale * math.log2(math.e)
    causal = lax.broadcasted_iota(jnp.int32, (BLK, BLK), 0) >= (
        lax.broadcasted_iota(jnp.int32, (BLK, BLK), 1)
    )

    def attend(h, then=None):
        cols = pl.ds(pl.multiple_of(h * HD, HD), HD)

        @pl.loop(1, n)
        def _(d):
            src = lax.rem(me + d, n)
            block_copy(src, src, h).wait_recv()

        if then:
            then(h)
        stage[...] = ids_in[:, h]
        for t in range(tiles):
            rows = slice(t * BLK, (t + 1) * BLK)
            span = (t + 1) * BLK
            owners = [ids_s[t, j] // mb_dev for j in range(topk)]
            keys = jnp.concatenate(
                [stage[o, 0] for o in owners] + [lkv[0, 0:span, cols]], axis=0
            )
            vals = jnp.concatenate(
                [stage[o, 1] for o in owners] + [lkv[1, 0:span, cols]], axis=0
            )
            s = dot_nt(qb[rows, cols], keys)
            dp = dot_nt(go[rows, cols], vals)
            edge = s.shape[1] - BLK
            s = jnp.concatenate(
                [s[:, :edge], jnp.where(causal, s[:, edge:], NEG_FILL)], axis=1
            )
            top = jnp.max(s, axis=1, keepdims=True)
            e = jnp.exp2((s - top) * rate)
            inv = 1.0 / jnp.sum(e, axis=1, keepdims=True)
            att_ref[rows, cols] = (dot_nn(e.astype(jnp.bfloat16), vals) * inv).astype(
                jnp.bfloat16
            )
            delta = jnp.sum(e * dp, axis=1, keepdims=True) * inv
            ds = (e * (dp - delta)).astype(jnp.bfloat16)
            gq[rows, cols] = (dot_nn(ds, keys) * (inv * scale)).astype(jnp.bfloat16)

    groups = n // per

    def span_of(g):
        return pl.ds(g * per, per)

    own_half = pl.ds(pl.multiple_of(cc * rows_dev, rows_dev), rows_dev)
    sib_half = pl.ds(pl.multiple_of((1 - cc) * rows_dev, rows_dev), rows_dev)

    def rs_s(d, g):
        return remote(
            part.at[d, span_of(g), sib_half, :], s_recv.at[d, span_of(g)],
            r_ssend.at[d, g], r_srecv.at[d, g], me, sib,
        )

    def rs_y(d, g):
        return remote(
            y_send.at[d, span_of(g)], y_recv.at[d, span_of(g)],
            r_ysend.at[d, g], r_yrecv.at[d, g], me, lax.rem(mf + 2 * d, nf),
        )

    def shares(first, last, cols):
        def partial(d, g):
            chip = lax.rem(yy + d, ny)
            rows = pl.ds(pl.multiple_of(chip * 2 * rows_dev, 2 * rows_dev), 2 * rows_dev)
            for i in range(per):
                p = g * per + i
                part[d, p] = dot_nt(gq[rows, cols], wf[slot_of(p), :, cols]).astype(
                    jnp.bfloat16
                )
            rs_s(d, g).start()

        def pass_on(d, g):
            rs_s(d, g).wait_recv()
            for i in range(per):
                p = g * per + i
                y_send[d, p] = (
                    part[d, p, own_half, :].astype(jnp.float32)
                    + s_recv[d, p].astype(jnp.float32)
                ).astype(jnp.bfloat16)
            rs_y(d, g).start()

        lag = min(LAG, last - first)
        for d in range(1, ny):
            @pl.loop(first, last + lag)
            def _(g):
                @pl.when(g < last)
                def _():
                    partial(d, g)

                @pl.when(g >= first + lag)
                def _():
                    pass_on(d, g - lag)

        @pl.loop(first, last)
        def _(g):
            partial(0, g)

    def settled(p):
        total = part[0, p, own_half, :].astype(jnp.float32) + s_recv[0, p].astype(jnp.float32)
        for d in range(1, ny):
            total = total + y_recv[d, p].astype(jnp.float32)
        return total

    def g_copy(f, src):
        return remote(
            gq.at[rows_of(f), late_cols], gq_in.at[src], g_send.at[f], g_recv.at[src], me, f
        )

    def resume(h):
        @pl.when(h == early - 1)
        def _():
            for late_head in range(early, heads):
                send_crossing(late_head)

    @pl.loop(0, early)
    def _(h):
        attend(h, resume)

    shares(0, swap // per, halves[0])

    for k in range(2, nz):
        at_distance(k, arrived(0, 1))
    for r in range(1, nx - 1):
        for k in range(nz):
            at_distance(k, arrived(r, 1))
    qb[:, late_cols] = q32[:, late_cols].astype(jnp.bfloat16)

    for d in range(1, ny):
        f = lax.rem(mf + 2 * d, nf)

        @pl.loop(0, swap)
        def _(p):
            v_fwd(f, p).wait_recv()
            v_fwd(f, p).start()

    @pl.loop(early, heads)
    def _(h):
        attend(h)

    for d in range(1, nf):
        g_copy(lax.rem(mf + d, nf), mf).start()
    c_att = pltpu.make_async_copy(att_ref, att_hbm, o_sem.at[n])
    c_att.start()

    def out_copy(p):
        return pltpu.make_async_copy(
            gin_ref.at[:, out_cols(p)], gin_hbm.at[:, out_cols(p)], o_sem.at[p]
        )

    shares(swap // per, groups, slice(0, width))

    for d in range(ny):
        f = lax.rem(sib + 2 * d, nf)

        @pl.loop(0, swap)
        def _(p):
            v_fwd(f, p).wait_recv()

    for d in range(1, nf):
        f = lax.rem(mf + d, nf)
        g_copy(f, f).wait_recv()

    def finish(g):
        rs_s(0, g).wait_recv()
        for d in range(1, ny):
            rs_y(d, g).wait_recv()

    def out_cols(p):
        return pl.ds(pl.multiple_of(slot_of(p) * dk, dk), dk)

    def gathered(p):
        total = dot_nt(gq[rows_of(mf), late_cols], wf[slot_of(p), :, late_cols])
        for d in range(1, nf):
            f = lax.rem(mf + d, nf)
            total = total + dot_nt(gq_in[f], wy[f, p])
        return total

    @pl.loop(0, swap // per)
    def _(g):
        finish(g)
        for i in range(per):
            p = g * per + i
            gin_ref[:, out_cols(p)] = (settled(p) + gathered(p)).astype(jnp.bfloat16)
            out_copy(p).start()

    @pl.loop(swap // per, groups)
    def _(g):
        finish(g)
        for i in range(per):
            p = g * per + i
            gin_ref[:, out_cols(p)] = settled(p).astype(jnp.bfloat16)
            out_copy(p).start()

    @pl.loop(1, n)
    def _(d):
        peer = lax.rem(me + d, n)
        id_copy(peer, me).wait_send()
        for h in range(heads):
            block_copy(peer, me, h).wait_send()

    @pl.loop(0, nz)
    def _(zz):
        for c in range(2):
            @pl.when((zz <= z) & (z + 1 < nz))
            def _():
                w_up_copy(zz, c).wait_send()

            @pl.when((zz >= z) & (z > 0))
            def _():
                w_down_copy(zz, c).wait_send()

            for r in range(nx - 1):
                w_x_copy(r, zz, c).wait_send()

    for d in range(ny):
        if d:
            x_ycopy(d).wait_send()
        x_scopy(lax.rem(mf + 2 * d, nf)).wait_send()

        @pl.loop(0, groups)
        def _(g):
            rs_s(d, g).wait_send()
            if d:
                rs_y(d, g).wait_send()

    @pl.loop(0, swap)
    def _(p):
        for d in range(1, ny):
            v_ycopy(d, p).wait_send()
            v_fwd(lax.rem(mf + 2 * d, nf), p).wait_send()
        v_own(p).wait_send()

    for d in range(1, nf):
        g_copy(lax.rem(mf + d, nf), mf).wait_send()

    c_att.wait()

    @pl.loop(0, n)
    def _(p):
        out_copy(p).wait()


def emit(a_ref, b_ref, c_ref, d_ref):
    c_ref[...] = a_ref[...]
    d_ref[...] = b_ref[...]


def local(n, nf, layer_input, w_query, local_kv, memory_kv, memory_ids, grad_out):
    nx = 2 ** ((n.bit_length() - 1) // 2)
    nz = n // nx
    ny = nf // 2
    rows_dev, d_model = layer_input.shape
    dk, width = w_query.shape
    ctx = rows_dev * nf
    mb_dev = memory_kv.shape[0]
    bf, f32, i32 = jnp.bfloat16, jnp.float32, jnp.int32
    any_spec = pl.BlockSpec(memory_space=pl.ANY)
    vmem_spec = pl.BlockSpec(memory_space=pltpu.VMEM)
    dma = pltpu.SemaphoreType.DMA
    heads = width // HD
    early = heads // 2
    per = max(1, nz // 4)
    groups = n // per
    lw = width - early * HD
    swap = min(nz + 2, n)
    blocks = pltpu.VMEM((n, heads, 2, BLK, HD), bf)
    piece = pltpu.VMEM((ny, n, rows_dev, dk), bf)
    outs = (
        jax.ShapeDtypeStruct((ctx, width), bf),
        jax.ShapeDtypeStruct((rows_dev, d_model), bf),
    )
    raw = pl.pallas_call(
        functools.partial(kernel, n, nx, nf, mb_dev, early, per, swap),
        out_shape=outs,
        in_specs=[pl.BlockSpec(memory_space=pltpu.SMEM), vmem_spec] + [any_spec] * 5,
        out_specs=(any_spec, any_spec),
        scratch_shapes=[
            pltpu.VMEM((n, dk, width), bf),
            pltpu.VMEM((ctx, d_model), bf),
            pltpu.VMEM(memory_kv.shape, bf),
            pltpu.VMEM(local_kv.shape, bf),
            pltpu.VMEM(grad_out.shape, bf),
            blocks,
            pltpu.VMEM((n,) + memory_ids.shape, i32),
            pltpu.VMEM((n, 2, BLK, HD), bf),
            blocks,
            pltpu.SMEM((n,) + memory_ids.shape, i32),
            pltpu.VMEM((ctx, width), f32),
            pltpu.VMEM((ctx, width), bf),
            pltpu.VMEM((ctx, width), bf),
            pltpu.VMEM((ny, n, 2 * rows_dev, dk), bf), piece, piece, piece,
            pltpu.VMEM((nf, swap, dk, lw), bf),
            pltpu.VMEM((nf, rows_dev, lw), bf),
            dma((5,)), dma((n,)), dma((n,)), dma((1,)),
            dma((nz, 2)), dma((nz, 2)), dma((max(nx - 1, 1), nz, 2)), dma((nz, 2)),
            dma((max(nx - 1, 1), nz, 2)),
            dma((ny,)), dma((nf,)), dma((nf,)), dma((n, heads)), dma((n, heads)),
            dma((ny, groups)), dma((ny, groups)), dma((ny, groups)), dma((ny, groups)),
            dma((ny, swap)), dma((nf, swap)), dma((nf, swap)),
            dma((nf,)), dma((nf,)), pltpu.SemaphoreType.REGULAR((3,)),
            pltpu.VMEM((ctx, width), bf), pltpu.VMEM((rows_dev, d_model), bf), dma((n + 1,)),
        ],
        compiler_params=pltpu.CompilerParams(
            collective_id=0, has_side_effects=True, vmem_limit_bytes=62 * 1024 * 1024
        ),
    )(memory_ids, memory_ids, layer_input, w_query, local_kv, memory_kv, grad_out)
    return pl.pallas_call(emit, out_shape=outs)(*raw)


def solution(mesh):
    placed = (
        P(("mem", "fsdp"), None),
        P("mem", "fsdp"),
        P(None, "mem", "fsdp"),
        P("mem", None, None, "fsdp"),
        P("mem", None),
        P("mem", "fsdp"),
    )
    return jax.shard_map(
        functools.partial(local, mesh.shape["mem"], mesh.shape["fsdp"]),
        mesh=mesh,
        in_specs=placed,
        out_specs=(P("mem", "fsdp"), P(("mem", "fsdp"), None)),
        check_vma=False,
    )
```

```python
import functools
import math

import jax
import jax.numpy as jnp
from jax import lax
from jax.experimental import pallas as pl
from jax.experimental.pallas import tpu as pltpu
from jax.sharding import PartitionSpec as P

HD = 128
BLK = 128
NEG_FILL = -1e30
LAG = 3
MESH = pl.DeviceIdType.MESH
NT = (((1,), (1,)), ((), ()))


def dot_nn(a, b):
    return jnp.dot(a, b, preferred_element_type=jnp.float32)


def dot_nt(a, b):
    return lax.dot_general(a, b, NT, preferred_element_type=jnp.float32)


def kernel(
    n, nx, nf, mb_dev, early, per, swap,
    ids_s, ids_v, x_hbm, w_hbm, lkv_hbm, mkv_hbm, go_hbm,
    att_hbm, gin_hbm,
    wf, xf, kv, lkv, go, outbox, inbox, stage, ids_in, ids_sm, q32, qb, gq,
    part, s_recv, y_send, y_recv, wy, gq_in,
    l_sem, i_send, i_recv, i_loc, w_up, w_down, w_x, w_recv, wx_recv,
    x_ysend, x_ssend, x_recv, m_send, m_recv, r_ssend, r_srecv, r_ysend, r_yrecv,
    v_ysend, v_ssend, v_recv, g_send, g_recv, seen, att_ref, gin_ref, o_sem,
):
    me = lax.axis_index("mem")
    mf = lax.axis_index("fsdp")
    nz = n // nx
    z, xx = me // nx, lax.rem(me, nx)
    ny = nf // 2
    yy, cc = mf // 2, lax.rem(mf, 2)
    sib = mf + 1 - 2 * cc
    dk = wf.shape[1]
    width = wf.shape[2]
    heads = width // HD
    tiles, topk = ids_s.shape
    rows_dev = xf.shape[0] // nf
    late = early * HD
    late_cols = slice(late, width)
    halves = (slice(0, late), late_cols)

    def local_copy(src, dst, k):
        return pltpu.make_async_copy(src, dst, l_sem.at[k])

    def rows_of(f):
        return pl.ds(pl.multiple_of(f * rows_dev, rows_dev), rows_dev)

    c_w = local_copy(w_hbm, wf.at[me], 0)
    c_x = local_copy(x_hbm, xf.at[rows_of(mf), :], 1)
    c_kv = local_copy(mkv_hbm, kv, 2)
    c_lkv = local_copy(lkv_hbm, lkv, 3)
    c_go = local_copy(go_hbm, go, 4)
    c_w.start()
    c_x.start()
    c_kv.start()
    c_lkv.start()
    c_go.start()

    barrier = pltpu.get_barrier_semaphore()

    x_next = z * nx + lax.rem(xx + 1, nx)
    x_prev = z * nx + lax.rem(xx + nx - 1, nx)
    below, above = z > 0, z + 1 < nz

    def signal(sem, dm, df):
        pl.semaphore_signal(sem, inc=1, device_id=(dm, df), device_id_type=MESH)

    @pl.when(above)
    def _():
        signal(barrier, me + nx, mf)

    @pl.when(below)
    def _():
        signal(barrier, me - nx, mf)

    signal(barrier, x_next, mf)
    if nx > 2:
        signal(barrier, x_prev, mf)
    for d in range(1, nf):
        signal(barrier, me, lax.rem(mf + d, nf))
    line = (z + nz - 2) // (nz - 1) + (2 * nz - 3 - z) // (nz - 1)
    pl.semaphore_wait(barrier, (1 if nx == 2 else 2) + nf - 1 + line)

    def remote(src, dst, s, r, dm, df):
        return pltpu.make_async_remote_copy(
            src_ref=src, dst_ref=dst, send_sem=s, recv_sem=r,
            device_id=(dm, df), device_id_type=MESH,
        )

    def id_copy(peer, slot):
        return remote(ids_v, inbox.at[slot], i_send.at[peer], i_recv.at[slot], peer, mf)

    def w_copy(slot, c, sem, dst_m, rsem):
        piece = wf.at[slot, :, halves[c]]
        return remote(piece, piece, sem, rsem, dst_m, mf)

    def w_up_copy(zz, c):
        return w_copy(zz * nx + xx, c, w_up.at[zz, c], me + nx, w_recv.at[zz, c])

    def w_down_copy(zz, c):
        return w_copy(zz * nx + xx, c, w_down.at[zz, c], me - nx, w_recv.at[zz, c])

    def w_x_copy(r, zz, c):
        slot = zz * nx + lax.rem(xx - r + nx, nx)
        return w_copy(slot, c, w_x.at[r, zz, c], x_next, wx_recv.at[r, zz, c])

    def w_x_arrival(r, zz, c):
        slot = zz * nx + lax.rem(xx - 1 - r + 2 * nx, nx)
        return w_copy(slot, c, w_x.at[r, zz, c], x_next, wx_recv.at[r, zz, c])

    turn = 1 - 2 * ((z + 1) // nz)

    def slot_of(p):
        return lax.rem(z + turn * lax.rem(p, nz) + nz, nz) * nx + lax.rem(xx - p // nz + nx, nx)

    def v_first(p, s, df):
        return remote(
            wf.at[slot_of(p), :, late_cols], wy.at[mf, p], s, v_recv.at[mf, p], me, df
        )

    def v_ycopy(d, p):
        return v_first(p, v_ysend.at[d, p], lax.rem(mf + 2 * d, nf))

    def v_own(p):
        return v_first(p, v_ssend.at[mf, p], sib)

    def v_fwd(f, p):
        return remote(
            wy.at[f, p], wy.at[f, p], v_ssend.at[f, p], v_recv.at[f, p], me, sib
        )

    def v_start(p):
        for d in range(1, ny):
            v_ycopy(d, p).start()
        v_own(p).start()

    c_w.wait()

    def w_begin(c):
        @pl.when(above)
        def _():
            w_up_copy(z, c).start()

        @pl.when(below)
        def _():
            w_down_copy(z, c).start()

        w_x_copy(0, z, c).start()

    w_begin(0)

    @pl.when(below)
    def _():
        pl.semaphore_wait(seen.at[0], 1)

    @pl.when(above)
    def _():
        signal(seen.at[0], me + nx, mf)
        pl.semaphore_wait(seen.at[1], 1)

    @pl.when(below)
    def _():
        signal(seen.at[1], me - nx, mf)

    for r in range(nx - 1):
        signal(seen.at[2], x_next, mf)
        pl.semaphore_wait(seen.at[2], 1)

    @pl.loop(1, n)
    def _(d):
        id_copy(lax.rem(me + d, n), me).start()

    w_begin(1)
    c_x.wait()

    def x_ycopy(d):
        return remote(
            xf.at[rows_of(mf), :], xf.at[rows_of(mf), :], x_ysend.at[d], x_recv.at[mf],
            me, lax.rem(mf + 2 * d, nf),
        )

    def x_scopy(f):
        return remote(
            xf.at[rows_of(f), :], xf.at[rows_of(f), :], x_ssend.at[f], x_recv.at[f], me, sib
        )

    for d in range(1, ny):
        x_ycopy(d).start()
    x_scopy(mf).start()
    v_start(0)

    def head_slice(h):
        return slice(h * HD, (h + 1) * HD)

    def fill():
        @pl.loop(1, n)
        def _(d):
            src = lax.rem(me + d, n)
            id_copy(src, src).wait_recv()

        c_ids = pltpu.make_async_copy(inbox, ids_sm, i_loc.at[0])
        c_ids.start()
        c_kv.wait()
        c_ids.wait()

        @pl.loop(1, n)
        def _(d):
            peer = lax.rem(me + d, n)
            want = jnp.int32(0)
            for j in range(tiles * topk):
                one = ids_sm[peer, j // topk, j % topk]
                want = jnp.where(one // mb_dev == me, lax.rem(one, mb_dev), want)
            for h in range(heads):
                outbox[peer, h] = kv[want, :, :, head_slice(h)]

        mine = jnp.int32(0)
        for j in range(tiles * topk):
            one = ids_s[j // topk, j % topk]
            mine = jnp.where(one // mb_dev == me, lax.rem(one, mb_dev), mine)
        for h in range(heads):
            ids_in[me, h] = kv[mine, :, :, head_slice(h)]

    def block_copy(peer, slot, h):
        return remote(
            outbox.at[peer, h], ids_in.at[slot, h], m_send.at[peer, h], m_recv.at[slot, h],
            peer, mf,
        )

    def send_blocks(hs, wanted):
        for h in hs:
            @pl.loop(1, n)
            def _(d):
                peer = lax.rem(me + n - d, n)

                @pl.when(wanted(peer // nx, lax.rem(peer, nx)))
                def _():
                    block_copy(peer, me, h).start()

    def send_crossing(h):
        send_blocks((h,), lambda pz, px: px != xx)

    def inner(pz):
        return (pz > 0) & (pz < nz - 1)

    for k in range(1, nz):
        for c in range(2):
            @pl.when(z - k >= 0)
            def _():
                w_up_copy(z - k, c).wait_recv()

                @pl.when(z + 1 < nz)
                def _():
                    w_up_copy(z - k, c).start()

                if c:
                    v_start(nz - k + (2 * k - nz) * ((z + 1) // nz))
                if c == 0 or k < 2:
                    w_x_copy(0, z - k, c).start()

            @pl.when(z + k < nz)
            def _():
                w_down_copy(z + k, c).wait_recv()

                @pl.when(z > 0)
                def _():
                    w_down_copy(z + k, c).start()

                if c:
                    v_start(k)
                if c == 0 or k < 2:
                    w_x_copy(0, z + k, c).start()

        if k == 1:
            fill()
        if k == min(2, nz - 1):
            send_blocks(range(heads), lambda pz, px: (px == xx) & inner(pz))
            for d in range(1, ny):
                f = lax.rem(mf + 2 * d, nf)
                x_scopy(f).wait_recv()
                x_scopy(f).start()


    for d in range(ny):
        x_scopy(lax.rem(sib + 2 * d, nf)).wait_recv()

    q32[...] = jnp.zeros_like(q32)

    def project(slot, c):
        q32[:, halves[c]] += dot_nn(
            xf[:, pl.ds(pl.multiple_of(slot * dk, dk), dk)], wf[slot, :, halves[c]]
        )

    def at_distance(k, body):
        for zz in (z - k, z + k) if k else (z,):
            @pl.when((zz >= 0) & (zz < nz))
            def _():
                body(zz)

    def arrived(r, c):
        def body(zz):
            w_x_arrival(r, zz, c).wait_recv()
            if r + 1 < nx - 1:
                w_x_copy(r + 1, zz, c).start()
            project(zz * nx + lax.rem(xx - 1 - r + 2 * nx, nx), c)

        return body

    def own_column(c):
        @pl.loop(0, nz)
        def _(zz):
            project(zz * nx + xx, c)

    def send_outer(hs):
        send_blocks(hs, lambda pz, px: (px == xx) & jnp.logical_not(inner(pz)))

    own_column(0)
    for r in range(nx - 1):
        for k in range(nz):
            at_distance(k, arrived(r, 0))
            if r == nx - 2 and k == 1:
                send_outer(range(early))
    for h in range(early):
        send_crossing(h)
    for k in range(2, nz):
        at_distance(k, lambda zz: w_x_copy(0, zz, 1).start())
    send_outer(range(early, heads))
    qb[:, halves[0]] = q32[:, halves[0]].astype(jnp.bfloat16)

    own_column(1)
    for k in range(min(2, nz)):
        at_distance(k, arrived(0, 1))
    for p in range(nz, swap):
        v_start(p)
    c_lkv.wait()
    c_go.wait()

    scale = 1.0 / math.sqrt(HD)
    rate = scale * math.log2(math.e)
    causal = lax.broadcasted_iota(jnp.int32, (BLK, BLK), 0) >= (
        lax.broadcasted_iota(jnp.int32, (BLK, BLK), 1)
    )

    def attend(h, then=None):
        cols = pl.ds(pl.multiple_of(h * HD, HD), HD)

        @pl.loop(1, n)
        def _(d):
            src = lax.rem(me + d, n)
            block_copy(src, src, h).wait_recv()

        if then:
            then(h)
        stage[...] = ids_in[:, h]
        for t in range(tiles):
            rows = slice(t * BLK, (t + 1) * BLK)
            span = (t + 1) * BLK
            owners = [ids_s[t, j] // mb_dev for j in range(topk)]
            keys = jnp.concatenate(
                [stage[o, 0] for o in owners] + [lkv[0, 0:span, cols]], axis=0
            )
            vals = jnp.concatenate(
                [stage[o, 1] for o in owners] + [lkv[1, 0:span, cols]], axis=0
            )
            s = dot_nt(qb[rows, cols], keys)
            dp = dot_nt(go[rows, cols], vals)
            edge = s.shape[1] - BLK
            s = jnp.concatenate(
                [s[:, :edge], jnp.where(causal, s[:, edge:], NEG_FILL)], axis=1
            )
            top = jnp.max(s, axis=1, keepdims=True)
            e = jnp.exp2((s - top) * rate)
            inv = 1.0 / jnp.sum(e, axis=1, keepdims=True)
            att_ref[rows, cols] = (dot_nn(e.astype(jnp.bfloat16), vals) * inv).astype(
                jnp.bfloat16
            )
            delta = jnp.sum(e * dp, axis=1, keepdims=True) * inv
            ds = (e * (dp - delta)).astype(jnp.bfloat16)
            gq[rows, cols] = (dot_nn(ds, keys) * (inv * scale)).astype(jnp.bfloat16)

    groups = n // per

    def span_of(g):
        return pl.ds(g * per, per)

    own_half = pl.ds(pl.multiple_of(cc * rows_dev, rows_dev), rows_dev)
    sib_half = pl.ds(pl.multiple_of((1 - cc) * rows_dev, rows_dev), rows_dev)

    def rs_s(d, g):
        return remote(
            part.at[d, span_of(g), sib_half, :], s_recv.at[d, span_of(g)],
            r_ssend.at[d, g], r_srecv.at[d, g], me, sib,
        )

    def rs_y(d, g):
        return remote(
            y_send.at[d, span_of(g)], y_recv.at[d, span_of(g)],
            r_ysend.at[d, g], r_yrecv.at[d, g], me, lax.rem(mf + 2 * d, nf),
        )

    def shares(first, last, cols):
        def partial(d, g):
            chip = lax.rem(yy + d, ny)
            rows = pl.ds(pl.multiple_of(chip * 2 * rows_dev, 2 * rows_dev), 2 * rows_dev)
            for i in range(per):
                p = g * per + i
                part[d, p] = dot_nt(gq[rows, cols], wf[slot_of(p), :, cols]).astype(
                    jnp.bfloat16
                )
            rs_s(d, g).start()

        def pass_on(d, g):
            rs_s(d, g).wait_recv()
            for i in range(per):
                p = g * per + i
                y_send[d, p] = (
                    part[d, p, own_half, :].astype(jnp.float32)
                    + s_recv[d, p].astype(jnp.float32)
                ).astype(jnp.bfloat16)
            rs_y(d, g).start()

        lag = min(LAG, last - first)
        for d in range(1, ny):
            @pl.loop(first, last + lag)
            def _(g):
                @pl.when(g < last)
                def _():
                    partial(d, g)

                @pl.when(g >= first + lag)
                def _():
                    pass_on(d, g - lag)

        @pl.loop(first, last)
        def _(g):
            partial(0, g)

    def settled(p):
        total = part[0, p, own_half, :].astype(jnp.float32) + s_recv[0, p].astype(jnp.float32)
        for d in range(1, ny):
            total = total + y_recv[d, p].astype(jnp.float32)
        return total

    def g_copy(f, src):
        return remote(
            gq.at[rows_of(f), late_cols], gq_in.at[src], g_send.at[f], g_recv.at[src], me, f
        )

    def resume(h):
        @pl.when(h == early - 1)
        def _():
            for late_head in range(early, heads):
                send_crossing(late_head)

    @pl.loop(0, early)
    def _(h):
        attend(h, resume)

    shares(0, swap // per, halves[0])

    for k in range(2, nz):
        at_distance(k, arrived(0, 1))
    for r in range(1, nx - 1):
        for k in range(nz):
            at_distance(k, arrived(r, 1))
    qb[:, late_cols] = q32[:, late_cols].astype(jnp.bfloat16)

    for d in range(1, ny):
        f = lax.rem(mf + 2 * d, nf)

        @pl.loop(0, swap)
        def _(p):
            v_fwd(f, p).wait_recv()
            v_fwd(f, p).start()

    @pl.loop(early, heads)
    def _(h):
        attend(h)

    for d in range(1, nf):
        g_copy(lax.rem(mf + d, nf), mf).start()
    c_att = pltpu.make_async_copy(att_ref, att_hbm, o_sem.at[n])
    c_att.start()

    def out_copy(p):
        return pltpu.make_async_copy(
            gin_ref.at[:, out_cols(p)], gin_hbm.at[:, out_cols(p)], o_sem.at[p]
        )

    shares(swap // per, groups, slice(0, width))

    for d in range(ny):
        f = lax.rem(sib + 2 * d, nf)

        @pl.loop(0, swap)
        def _(p):
            v_fwd(f, p).wait_recv()

    for d in range(1, nf):
        f = lax.rem(mf + d, nf)
        g_copy(f, f).wait_recv()

    def finish(g):
        rs_s(0, g).wait_recv()
        for d in range(1, ny):
            rs_y(d, g).wait_recv()

    def out_cols(p):
        return pl.ds(pl.multiple_of(slot_of(p) * dk, dk), dk)

    def gathered(p):
        total = dot_nt(gq[rows_of(mf), late_cols], wf[slot_of(p), :, late_cols])
        for d in range(1, nf):
            f = lax.rem(mf + d, nf)
            total = total + dot_nt(gq_in[f], wy[f, p])
        return total

    @pl.loop(0, swap // per)
    def _(g):
        finish(g)
        for i in range(per):
            p = g * per + i
            gin_ref[:, out_cols(p)] = (settled(p) + gathered(p)).astype(jnp.bfloat16)
            out_copy(p).start()

    @pl.loop(swap // per, groups)
    def _(g):
        finish(g)
        for i in range(per):
            p = g * per + i
            gin_ref[:, out_cols(p)] = settled(p).astype(jnp.bfloat16)
            out_copy(p).start()

    @pl.loop(1, n)
    def _(d):
        peer = lax.rem(me + d, n)
        id_copy(peer, me).wait_send()
        for h in range(heads):
            block_copy(peer, me, h).wait_send()

    @pl.loop(0, nz)
    def _(zz):
        for c in range(2):
            @pl.when((zz <= z) & (z + 1 < nz))
            def _():
                w_up_copy(zz, c).wait_send()

            @pl.when((zz >= z) & (z > 0))
            def _():
                w_down_copy(zz, c).wait_send()

            for r in range(nx - 1):
                w_x_copy(r, zz, c).wait_send()

    for d in range(ny):
        if d:
            x_ycopy(d).wait_send()
        x_scopy(lax.rem(mf + 2 * d, nf)).wait_send()

        @pl.loop(0, groups)
        def _(g):
            rs_s(d, g).wait_send()
            if d:
                rs_y(d, g).wait_send()

    @pl.loop(0, swap)
    def _(p):
        for d in range(1, ny):
            v_ycopy(d, p).wait_send()
            v_fwd(lax.rem(mf + 2 * d, nf), p).wait_send()
        v_own(p).wait_send()

    for d in range(1, nf):
        g_copy(lax.rem(mf + d, nf), mf).wait_send()

    c_att.wait()

    @pl.loop(0, n)
    def _(p):
        out_copy(p).wait()


def emit(a_hbm, b_hbm, c_hbm, d_hbm, a, b, sem):
    steps = a.shape[0]
    jobs = []
    for i in range(steps):
        jobs.append((a_hbm.at[i], a.at[i], c_hbm.at[i]))
        jobs.append((b_hbm.at[i], b.at[i], d_hbm.at[i]))
    for j, (src, held, _) in enumerate(jobs):
        pltpu.make_async_copy(src, held, sem.at[0, j]).start()
    for j, (src, held, dst) in enumerate(jobs):
        pltpu.make_async_copy(src, held, sem.at[0, j]).wait()
        pltpu.make_async_copy(held, dst, sem.at[1, j]).start()
    for j, (_, held, dst) in enumerate(jobs):
        pltpu.make_async_copy(held, dst, sem.at[1, j]).wait()


def local(n, nf, layer_input, w_query, local_kv, memory_kv, memory_ids, grad_out):
    nx = 2 ** ((n.bit_length() - 1) // 2)
    nz = n // nx
    ny = nf // 2
    rows_dev, d_model = layer_input.shape
    dk, width = w_query.shape
    ctx = rows_dev * nf
    mb_dev = memory_kv.shape[0]
    bf, f32, i32 = jnp.bfloat16, jnp.float32, jnp.int32
    any_spec = pl.BlockSpec(memory_space=pl.ANY)
    vmem_spec = pl.BlockSpec(memory_space=pltpu.VMEM)
    dma = pltpu.SemaphoreType.DMA
    heads = width // HD
    early = heads // 2
    per = max(1, nz // 4)
    groups = n // per
    lw = width - early * HD
    swap = min(nz + 2, n)
    blocks = pltpu.VMEM((n, heads, 2, BLK, HD), bf)
    piece = pltpu.VMEM((ny, n, rows_dev, dk), bf)
    outs = (
        jax.ShapeDtypeStruct((ctx, width), bf),
        jax.ShapeDtypeStruct((rows_dev, d_model), bf),
    )
    raw = pl.pallas_call(
        functools.partial(kernel, n, nx, nf, mb_dev, early, per, swap),
        out_shape=outs,
        in_specs=[pl.BlockSpec(memory_space=pltpu.SMEM), vmem_spec] + [any_spec] * 5,
        out_specs=(any_spec, any_spec),
        scratch_shapes=[
            pltpu.VMEM((n, dk, width), bf),
            pltpu.VMEM((ctx, d_model), bf),
            pltpu.VMEM(memory_kv.shape, bf),
            pltpu.VMEM(local_kv.shape, bf),
            pltpu.VMEM(grad_out.shape, bf),
            blocks,
            pltpu.VMEM((n,) + memory_ids.shape, i32),
            pltpu.VMEM((n, 2, BLK, HD), bf),
            blocks,
            pltpu.SMEM((n,) + memory_ids.shape, i32),
            pltpu.VMEM((ctx, width), f32),
            pltpu.VMEM((ctx, width), bf),
            pltpu.VMEM((ctx, width), bf),
            pltpu.VMEM((ny, n, 2 * rows_dev, dk), bf), piece, piece, piece,
            pltpu.VMEM((nf, swap, dk, lw), bf),
            pltpu.VMEM((nf, rows_dev, lw), bf),
            dma((5,)), dma((n,)), dma((n,)), dma((1,)),
            dma((nz, 2)), dma((nz, 2)), dma((max(nx - 1, 1), nz, 2)), dma((nz, 2)),
            dma((max(nx - 1, 1), nz, 2)),
            dma((ny,)), dma((nf,)), dma((nf,)), dma((n, heads)), dma((n, heads)),
            dma((ny, groups)), dma((ny, groups)), dma((ny, groups)), dma((ny, groups)),
            dma((ny, swap)), dma((nf, swap)), dma((nf, swap)),
            dma((nf,)), dma((nf,)), pltpu.SemaphoreType.REGULAR((3,)),
            pltpu.VMEM((ctx, width), bf), pltpu.VMEM((rows_dev, d_model), bf), dma((n + 1,)),
        ],
        compiler_params=pltpu.CompilerParams(
            collective_id=0, has_side_effects=True, vmem_limit_bytes=62 * 1024 * 1024
        ),
    )(memory_ids, memory_ids, layer_input, w_query, local_kv, memory_kv, grad_out)
    steps = 4
    cut = [o.update(shape=(steps, o.shape[0] // steps) + o.shape[1:]) for o in outs]
    done = pl.pallas_call(
        emit,
        out_shape=cut,
        in_specs=[any_spec] * 2,
        out_specs=[any_spec] * 2,
        scratch_shapes=[pltpu.VMEM(c.shape, bf) for c in cut] + [dma((2, 2 * steps))],
    )(*[r.reshape(c.shape) for r, c in zip(raw, cut)])
    return tuple(x.reshape(o.shape) for x, o in zip(done, outs))


def solution(mesh):
    placed = (
        P(("mem", "fsdp"), None),
        P("mem", "fsdp"),
        P(None, "mem", "fsdp"),
        P("mem", None, None, "fsdp"),
        P("mem", None),
        P("mem", "fsdp"),
    )
    return jax.shard_map(
        functools.partial(local, mesh.shape["mem"], mesh.shape["fsdp"]),
        mesh=mesh,
        in_specs=placed,
        out_specs=(P("mem", "fsdp"), P(("mem", "fsdp"), None)),
        check_vma=False,
    )
```

```python
import functools
import math

import jax
import jax.numpy as jnp
from jax import lax
from jax.experimental import pallas as pl
from jax.experimental.pallas import tpu as pltpu
from jax.sharding import PartitionSpec as P

HD = 128
BLK = 128
NEG_FILL = -1e30
LAG = 2
MESH = pl.DeviceIdType.MESH
NT = (((1,), (1,)), ((), ()))


def dot_nn(a, b):
    return jnp.dot(a, b, preferred_element_type=jnp.float32)


def dot_nt(a, b):
    return lax.dot_general(a, b, NT, preferred_element_type=jnp.float32)


def kernel(
    n, nx, nf, mb_dev, early, per, swap,
    ids_s, ids_v, x_hbm, w_hbm, lkv_hbm, mkv_hbm, go_hbm,
    att_hbm, gin_hbm,
    wf, xf, kv, lkv, go, outbox, inbox, stage, ids_in, ids_sm, q32, qb, gq,
    part, s_recv, y_send, y_recv, wy, gq_in,
    l_sem, i_send, i_recv, i_loc, w_up, w_down, w_x, w_recv, wx_recv,
    x_ysend, x_ssend, x_recv, m_send, m_recv, r_ssend, r_srecv, r_ysend, r_yrecv,
    v_ysend, v_ssend, v_recv, g_send, g_recv, seen, att_ref, gin_ref, o_sem,
):
    me = lax.axis_index("mem")
    mf = lax.axis_index("fsdp")
    nz = n // nx
    z, xx = me // nx, lax.rem(me, nx)
    ny = nf // 2
    yy, cc = mf // 2, lax.rem(mf, 2)
    sib = mf + 1 - 2 * cc
    dk = wf.shape[1]
    width = wf.shape[2]
    heads = width // HD
    tiles, topk = ids_s.shape
    rows_dev = xf.shape[0] // nf
    late = early * HD
    late_cols = slice(late, width)
    halves = (slice(0, late), late_cols)

    def local_copy(src, dst, k):
        return pltpu.make_async_copy(src, dst, l_sem.at[k])

    def rows_of(f):
        return pl.ds(pl.multiple_of(f * rows_dev, rows_dev), rows_dev)

    c_w = local_copy(w_hbm, wf.at[me], 0)
    c_x = local_copy(x_hbm, xf.at[rows_of(mf), :], 1)
    c_kv = local_copy(mkv_hbm, kv, 2)
    c_lkv = local_copy(lkv_hbm, lkv, 3)
    c_go = local_copy(go_hbm, go, 4)
    c_w.start()
    c_x.start()
    c_kv.start()
    c_lkv.start()
    c_go.start()

    barrier = pltpu.get_barrier_semaphore()

    x_next = z * nx + lax.rem(xx + 1, nx)
    x_prev = z * nx + lax.rem(xx + nx - 1, nx)
    below, above = z > 0, z + 1 < nz

    def signal(sem, dm, df):
        pl.semaphore_signal(sem, inc=1, device_id=(dm, df), device_id_type=MESH)

    @pl.when(above)
    def _():
        signal(barrier, me + nx, mf)

    @pl.when(below)
    def _():
        signal(barrier, me - nx, mf)

    signal(barrier, x_next, mf)
    if nx > 2:
        signal(barrier, x_prev, mf)
    for d in range(1, nf):
        signal(barrier, me, lax.rem(mf + d, nf))
    line = (z + nz - 2) // (nz - 1) + (2 * nz - 3 - z) // (nz - 1)
    pl.semaphore_wait(barrier, (1 if nx == 2 else 2) + nf - 1 + line)

    def remote(src, dst, s, r, dm, df):
        return pltpu.make_async_remote_copy(
            src_ref=src, dst_ref=dst, send_sem=s, recv_sem=r,
            device_id=(dm, df), device_id_type=MESH,
        )

    def id_copy(peer, slot):
        return remote(ids_v, inbox.at[slot], i_send.at[peer], i_recv.at[slot], peer, mf)

    def w_copy(slot, c, sem, dst_m, rsem):
        piece = wf.at[slot, :, halves[c]]
        return remote(piece, piece, sem, rsem, dst_m, mf)

    def w_up_copy(zz, c):
        return w_copy(zz * nx + xx, c, w_up.at[zz, c], me + nx, w_recv.at[zz, c])

    def w_down_copy(zz, c):
        return w_copy(zz * nx + xx, c, w_down.at[zz, c], me - nx, w_recv.at[zz, c])

    def w_x_copy(r, zz, c):
        slot = zz * nx + lax.rem(xx - r + nx, nx)
        return w_copy(slot, c, w_x.at[r, zz, c], x_next, wx_recv.at[r, zz, c])

    def w_x_arrival(r, zz, c):
        slot = zz * nx + lax.rem(xx - 1 - r + 2 * nx, nx)
        return w_copy(slot, c, w_x.at[r, zz, c], x_next, wx_recv.at[r, zz, c])

    turn = 1 - 2 * ((z + 1) // nz)

    def slot_of(p):
        return lax.rem(z + turn * lax.rem(p, nz) + nz, nz) * nx + lax.rem(xx - p // nz + nx, nx)

    def v_first(p, s, df):
        return remote(
            wf.at[slot_of(p), :, late_cols], wy.at[mf, p], s, v_recv.at[mf, p], me, df
        )

    def v_ycopy(d, p):
        return v_first(p, v_ysend.at[d, p], lax.rem(mf + 2 * d, nf))

    def v_own(p):
        return v_first(p, v_ssend.at[mf, p], sib)

    def v_fwd(f, p):
        return remote(
            wy.at[f, p], wy.at[f, p], v_ssend.at[f, p], v_recv.at[f, p], me, sib
        )

    def v_start(p):
        for d in range(1, ny):
            v_ycopy(d, p).start()
        v_own(p).start()

    c_w.wait()

    def w_begin(c):
        @pl.when(above)
        def _():
            w_up_copy(z, c).start()

        @pl.when(below)
        def _():
            w_down_copy(z, c).start()

        w_x_copy(0, z, c).start()

    w_begin(0)

    @pl.when(below)
    def _():
        pl.semaphore_wait(seen.at[0], 1)

    @pl.when(above)
    def _():
        signal(seen.at[0], me + nx, mf)
        pl.semaphore_wait(seen.at[1], 1)

    @pl.when(below)
    def _():
        signal(seen.at[1], me - nx, mf)

    for r in range(nx - 1):
        signal(seen.at[2], x_next, mf)
        pl.semaphore_wait(seen.at[2], 1)

    @pl.loop(1, n)
    def _(d):
        id_copy(lax.rem(me + d, n), me).start()

    w_begin(1)
    c_x.wait()

    def x_ycopy(d):
        return remote(
            xf.at[rows_of(mf), :], xf.at[rows_of(mf), :], x_ysend.at[d], x_recv.at[mf],
            me, lax.rem(mf + 2 * d, nf),
        )

    def x_scopy(f):
        return remote(
            xf.at[rows_of(f), :], xf.at[rows_of(f), :], x_ssend.at[f], x_recv.at[f], me, sib
        )

    for d in range(1, ny):
        x_ycopy(d).start()
    x_scopy(mf).start()
    v_start(0)

    def head_slice(h):
        return slice(h * HD, (h + 1) * HD)

    def fill():
        @pl.loop(1, n)
        def _(d):
            src = lax.rem(me + d, n)
            id_copy(src, src).wait_recv()

        c_ids = pltpu.make_async_copy(inbox, ids_sm, i_loc.at[0])
        c_ids.start()
        c_kv.wait()
        c_ids.wait()

        @pl.loop(1, n)
        def _(d):
            peer = lax.rem(me + d, n)
            want = jnp.int32(0)
            for j in range(tiles * topk):
                one = ids_sm[peer, j // topk, j % topk]
                want = jnp.where(one // mb_dev == me, lax.rem(one, mb_dev), want)
            for h in range(heads):
                outbox[peer, h] = kv[want, :, :, head_slice(h)]

        mine = jnp.int32(0)
        for j in range(tiles * topk):
            one = ids_s[j // topk, j % topk]
            mine = jnp.where(one // mb_dev == me, lax.rem(one, mb_dev), mine)
        for h in range(heads):
            ids_in[me, h] = kv[mine, :, :, head_slice(h)]

    def block_copy(peer, slot, h):
        return remote(
            outbox.at[peer, h], ids_in.at[slot, h], m_send.at[peer, h], m_recv.at[slot, h],
            peer, mf,
        )

    def send_blocks(hs, wanted):
        for h in hs:
            @pl.loop(1, n)
            def _(d):
                peer = lax.rem(me + n - d, n)

                @pl.when(wanted(peer // nx, lax.rem(peer, nx)))
                def _():
                    block_copy(peer, me, h).start()

    def send_crossing(h):
        send_blocks((h,), lambda pz, px: px != xx)

    def inner(pz):
        return (pz > 0) & (pz < nz - 1)

    for k in range(1, nz):
        for c in range(2):
            @pl.when(z - k >= 0)
            def _():
                w_up_copy(z - k, c).wait_recv()

                @pl.when(z + 1 < nz)
                def _():
                    w_up_copy(z - k, c).start()

                if c:
                    v_start(nz - k + (2 * k - nz) * ((z + 1) // nz))
                if c == 0 or k < 2:
                    w_x_copy(0, z - k, c).start()

            @pl.when(z + k < nz)
            def _():
                w_down_copy(z + k, c).wait_recv()

                @pl.when(z > 0)
                def _():
                    w_down_copy(z + k, c).start()

                if c:
                    v_start(k)
                if c == 0 or k < 2:
                    w_x_copy(0, z + k, c).start()

        if k == 1:
            fill()
        if k == min(2, nz - 1):
            send_blocks(range(heads), lambda pz, px: (px == xx) & inner(pz))
            for d in range(1, ny):
                f = lax.rem(mf + 2 * d, nf)
                x_scopy(f).wait_recv()
                x_scopy(f).start()


    for d in range(ny):
        x_scopy(lax.rem(sib + 2 * d, nf)).wait_recv()

    q32[...] = jnp.zeros_like(q32)

    def project(slot, c):
        q32[:, halves[c]] += dot_nn(
            xf[:, pl.ds(pl.multiple_of(slot * dk, dk), dk)], wf[slot, :, halves[c]]
        )

    def at_distance(k, body):
        for zz in (z - k, z + k) if k else (z,):
            @pl.when((zz >= 0) & (zz < nz))
            def _():
                body(zz)

    def arrived(r, c):
        def body(zz):
            w_x_arrival(r, zz, c).wait_recv()
            if r + 1 < nx - 1:
                w_x_copy(r + 1, zz, c).start()
            project(zz * nx + lax.rem(xx - 1 - r + 2 * nx, nx), c)

        return body

    def own_column(c):
        @pl.loop(0, nz)
        def _(zz):
            project(zz * nx + xx, c)

    def send_outer(hs):
        send_blocks(hs, lambda pz, px: (px == xx) & jnp.logical_not(inner(pz)))

    own_column(0)
    for r in range(nx - 1):
        for k in range(nz):
            at_distance(k, arrived(r, 0))
            if r == nx - 2 and k == 1:
                send_outer(range(early))
    for h in range(early):
        send_crossing(h)
    for k in range(2, nz):
        at_distance(k, lambda zz: w_x_copy(0, zz, 1).start())
    send_outer(range(early, heads))
    qb[:, halves[0]] = q32[:, halves[0]].astype(jnp.bfloat16)

    own_column(1)
    for k in range(min(2, nz)):
        at_distance(k, arrived(0, 1))
    for p in range(nz, swap):
        v_start(p)
    c_lkv.wait()
    c_go.wait()

    scale = 1.0 / math.sqrt(HD)
    rate = scale * math.log2(math.e)
    causal = lax.broadcasted_iota(jnp.int32, (BLK, BLK), 0) >= (
        lax.broadcasted_iota(jnp.int32, (BLK, BLK), 1)
    )

    def attend(h, then=None):
        cols = pl.ds(pl.multiple_of(h * HD, HD), HD)

        @pl.loop(1, n)
        def _(d):
            src = lax.rem(me + d, n)
            block_copy(src, src, h).wait_recv()

        if then:
            then(h)
        stage[...] = ids_in[:, h]
        for t in range(tiles):
            rows = slice(t * BLK, (t + 1) * BLK)
            span = (t + 1) * BLK
            owners = [ids_s[t, j] // mb_dev for j in range(topk)]
            keys = jnp.concatenate(
                [stage[o, 0] for o in owners] + [lkv[0, 0:span, cols]], axis=0
            )
            vals = jnp.concatenate(
                [stage[o, 1] for o in owners] + [lkv[1, 0:span, cols]], axis=0
            )
            s = dot_nt(qb[rows, cols], keys)
            dp = dot_nt(go[rows, cols], vals)
            edge = s.shape[1] - BLK
            s = jnp.concatenate(
                [s[:, :edge], jnp.where(causal, s[:, edge:], NEG_FILL)], axis=1
            )
            top = jnp.max(s, axis=1, keepdims=True)
            e = jnp.exp2((s - top) * rate)
            inv = 1.0 / jnp.sum(e, axis=1, keepdims=True)
            att_ref[rows, cols] = (dot_nn(e.astype(jnp.bfloat16), vals) * inv).astype(
                jnp.bfloat16
            )
            delta = jnp.sum(e * dp, axis=1, keepdims=True) * inv
            ds = (e * (dp - delta)).astype(jnp.bfloat16)
            gq[rows, cols] = (dot_nn(ds, keys) * (inv * scale)).astype(jnp.bfloat16)

    groups = n // per

    def span_of(g):
        return pl.ds(g * per, per)

    own_half = pl.ds(pl.multiple_of(cc * rows_dev, rows_dev), rows_dev)
    sib_half = pl.ds(pl.multiple_of((1 - cc) * rows_dev, rows_dev), rows_dev)

    def rs_s(d, g):
        return remote(
            part.at[d, span_of(g), sib_half, :], s_recv.at[d, span_of(g)],
            r_ssend.at[d, g], r_srecv.at[d, g], me, sib,
        )

    def rs_y(d, g):
        return remote(
            y_send.at[d, span_of(g)], y_recv.at[d, span_of(g)],
            r_ysend.at[d, g], r_yrecv.at[d, g], me, lax.rem(mf + 2 * d, nf),
        )

    def shares(first, last, cols):
        def partial(d, g):
            chip = lax.rem(yy + d, ny)
            rows = pl.ds(pl.multiple_of(chip * 2 * rows_dev, 2 * rows_dev), 2 * rows_dev)
            for i in range(per):
                p = g * per + i
                part[d, p] = dot_nt(gq[rows, cols], wf[slot_of(p), :, cols]).astype(
                    jnp.bfloat16
                )
            rs_s(d, g).start()

        def pass_on(d, g):
            rs_s(d, g).wait_recv()
            for i in range(per):
                p = g * per + i
                y_send[d, p] = (
                    part[d, p, own_half, :].astype(jnp.float32)
                    + s_recv[d, p].astype(jnp.float32)
                ).astype(jnp.bfloat16)
            rs_y(d, g).start()

        lag = min(LAG, last - first)
        for d in range(1, ny):
            @pl.loop(first, last + lag)
            def _(g):
                @pl.when(g < last)
                def _():
                    partial(d, g)

                @pl.when(g >= first + lag)
                def _():
                    pass_on(d, g - lag)

        @pl.loop(first, last)
        def _(g):
            partial(0, g)

    def settled(p):
        total = part[0, p, own_half, :].astype(jnp.float32) + s_recv[0, p].astype(jnp.float32)
        for d in range(1, ny):
            total = total + y_recv[d, p].astype(jnp.float32)
        return total

    def g_copy(f, src):
        return remote(
            gq.at[rows_of(f), late_cols], gq_in.at[src], g_send.at[f], g_recv.at[src], me, f
        )

    def resume(h):
        @pl.when(h == early - 1)
        def _():
            for late_head in range(early, heads):
                send_crossing(late_head)

    @pl.loop(0, early)
    def _(h):
        attend(h, resume)

    shares(0, swap // per, halves[0])

    for k in range(2, nz):
        at_distance(k, arrived(0, 1))
    for r in range(1, nx - 1):
        for k in range(nz):
            at_distance(k, arrived(r, 1))
    qb[:, late_cols] = q32[:, late_cols].astype(jnp.bfloat16)

    for d in range(1, ny):
        f = lax.rem(mf + 2 * d, nf)

        @pl.loop(0, swap)
        def _(p):
            v_fwd(f, p).wait_recv()
            v_fwd(f, p).start()

    @pl.loop(early, heads)
    def _(h):
        attend(h)

    for d in range(1, nf):
        g_copy(lax.rem(mf + d, nf), mf).start()
    c_att = pltpu.make_async_copy(att_ref, att_hbm, o_sem.at[n])
    c_att.start()

    def out_copy(p):
        return pltpu.make_async_copy(
            gin_ref.at[:, out_cols(p)], gin_hbm.at[:, out_cols(p)], o_sem.at[p]
        )

    shares(swap // per, groups, slice(0, width))

    for d in range(ny):
        f = lax.rem(sib + 2 * d, nf)

        @pl.loop(0, swap)
        def _(p):
            v_fwd(f, p).wait_recv()

    for d in range(1, nf):
        f = lax.rem(mf + d, nf)
        g_copy(f, f).wait_recv()

    def finish(g):
        rs_s(0, g).wait_recv()
        for d in range(1, ny):
            rs_y(d, g).wait_recv()

    def out_cols(p):
        return pl.ds(pl.multiple_of(slot_of(p) * dk, dk), dk)

    def gathered(p):
        total = dot_nt(gq[rows_of(mf), late_cols], wf[slot_of(p), :, late_cols])
        for d in range(1, nf):
            f = lax.rem(mf + d, nf)
            total = total + dot_nt(gq_in[f], wy[f, p])
        return total

    @pl.loop(0, swap // per)
    def _(g):
        finish(g)
        for i in range(per):
            p = g * per + i
            gin_ref[:, out_cols(p)] = (settled(p) + gathered(p)).astype(jnp.bfloat16)
            out_copy(p).start()

    @pl.loop(swap // per, groups)
    def _(g):
        finish(g)
        for i in range(per):
            p = g * per + i
            gin_ref[:, out_cols(p)] = settled(p).astype(jnp.bfloat16)
            out_copy(p).start()

    @pl.loop(1, n)
    def _(d):
        peer = lax.rem(me + d, n)
        id_copy(peer, me).wait_send()
        for h in range(heads):
            block_copy(peer, me, h).wait_send()

    @pl.loop(0, nz)
    def _(zz):
        for c in range(2):
            @pl.when((zz <= z) & (z + 1 < nz))
            def _():
                w_up_copy(zz, c).wait_send()

            @pl.when((zz >= z) & (z > 0))
            def _():
                w_down_copy(zz, c).wait_send()

            for r in range(nx - 1):
                w_x_copy(r, zz, c).wait_send()

    for d in range(ny):
        if d:
            x_ycopy(d).wait_send()
        x_scopy(lax.rem(mf + 2 * d, nf)).wait_send()

        @pl.loop(0, groups)
        def _(g):
            rs_s(d, g).wait_send()
            if d:
                rs_y(d, g).wait_send()

    @pl.loop(0, swap)
    def _(p):
        for d in range(1, ny):
            v_ycopy(d, p).wait_send()
            v_fwd(lax.rem(mf + 2 * d, nf), p).wait_send()
        v_own(p).wait_send()

    for d in range(1, nf):
        g_copy(lax.rem(mf + d, nf), mf).wait_send()

    c_att.wait()

    @pl.loop(0, n)
    def _(p):
        out_copy(p).wait()


def emit(a_hbm, b_hbm, c_hbm, d_hbm, a, b, sem):
    steps = a.shape[0]
    jobs = []
    for i in range(steps):
        jobs.append((a_hbm.at[i], a.at[i], c_hbm.at[i]))
        jobs.append((b_hbm.at[i], b.at[i], d_hbm.at[i]))
    for j, (src, held, _) in enumerate(jobs):
        pltpu.make_async_copy(src, held, sem.at[0, j]).start()
    for j, (src, held, dst) in enumerate(jobs):
        pltpu.make_async_copy(src, held, sem.at[0, j]).wait()
        pltpu.make_async_copy(held, dst, sem.at[1, j]).start()
    for j, (_, held, dst) in enumerate(jobs):
        pltpu.make_async_copy(held, dst, sem.at[1, j]).wait()


def local(n, nf, layer_input, w_query, local_kv, memory_kv, memory_ids, grad_out):
    nx = 2 ** ((n.bit_length() - 1) // 2)
    nz = n // nx
    ny = nf // 2
    rows_dev, d_model = layer_input.shape
    dk, width = w_query.shape
    ctx = rows_dev * nf
    mb_dev = memory_kv.shape[0]
    bf, f32, i32 = jnp.bfloat16, jnp.float32, jnp.int32
    any_spec = pl.BlockSpec(memory_space=pl.ANY)
    vmem_spec = pl.BlockSpec(memory_space=pltpu.VMEM)
    dma = pltpu.SemaphoreType.DMA
    heads = width // HD
    early = heads // 2
    per = max(1, nz // 4)
    groups = n // per
    lw = width - early * HD
    swap = min(nz + 2, n)
    blocks = pltpu.VMEM((n, heads, 2, BLK, HD), bf)
    piece = pltpu.VMEM((ny, n, rows_dev, dk), bf)
    outs = (
        jax.ShapeDtypeStruct((ctx, width), bf),
        jax.ShapeDtypeStruct((rows_dev, d_model), bf),
    )
    raw = pl.pallas_call(
        functools.partial(kernel, n, nx, nf, mb_dev, early, per, swap),
        out_shape=outs,
        in_specs=[pl.BlockSpec(memory_space=pltpu.SMEM), vmem_spec] + [any_spec] * 5,
        out_specs=(any_spec, any_spec),
        scratch_shapes=[
            pltpu.VMEM((n, dk, width), bf),
            pltpu.VMEM((ctx, d_model), bf),
            pltpu.VMEM(memory_kv.shape, bf),
            pltpu.VMEM(local_kv.shape, bf),
            pltpu.VMEM(grad_out.shape, bf),
            blocks,
            pltpu.VMEM((n,) + memory_ids.shape, i32),
            pltpu.VMEM((n, 2, BLK, HD), bf),
            blocks,
            pltpu.SMEM((n,) + memory_ids.shape, i32),
            pltpu.VMEM((ctx, width), f32),
            pltpu.VMEM((ctx, width), bf),
            pltpu.VMEM((ctx, width), bf),
            pltpu.VMEM((ny, n, 2 * rows_dev, dk), bf), piece, piece, piece,
            pltpu.VMEM((nf, swap, dk, lw), bf),
            pltpu.VMEM((nf, rows_dev, lw), bf),
            dma((5,)), dma((n,)), dma((n,)), dma((1,)),
            dma((nz, 2)), dma((nz, 2)), dma((max(nx - 1, 1), nz, 2)), dma((nz, 2)),
            dma((max(nx - 1, 1), nz, 2)),
            dma((ny,)), dma((nf,)), dma((nf,)), dma((n, heads)), dma((n, heads)),
            dma((ny, groups)), dma((ny, groups)), dma((ny, groups)), dma((ny, groups)),
            dma((ny, swap)), dma((nf, swap)), dma((nf, swap)),
            dma((nf,)), dma((nf,)), pltpu.SemaphoreType.REGULAR((3,)),
            pltpu.VMEM((ctx, width), bf), pltpu.VMEM((rows_dev, d_model), bf), dma((n + 1,)),
        ],
        compiler_params=pltpu.CompilerParams(
            collective_id=0, has_side_effects=True, vmem_limit_bytes=62 * 1024 * 1024
        ),
    )(memory_ids, memory_ids, layer_input, w_query, local_kv, memory_kv, grad_out)
    steps = 4
    cut = [o.update(shape=(steps, o.shape[0] // steps) + o.shape[1:]) for o in outs]
    done = pl.pallas_call(
        emit,
        out_shape=cut,
        in_specs=[any_spec] * 2,
        out_specs=[any_spec] * 2,
        scratch_shapes=[pltpu.VMEM(c.shape, bf) for c in cut] + [dma((2, 2 * steps))],
    )(*[r.reshape(c.shape) for r, c in zip(raw, cut)])
    return tuple(x.reshape(o.shape) for x, o in zip(done, outs))


def solution(mesh):
    placed = (
        P(("mem", "fsdp"), None),
        P("mem", "fsdp"),
        P(None, "mem", "fsdp"),
        P("mem", None, None, "fsdp"),
        P("mem", None),
        P("mem", "fsdp"),
    )
    return jax.shard_map(
        functools.partial(local, mesh.shape["mem"], mesh.shape["fsdp"]),
        mesh=mesh,
        in_specs=placed,
        out_specs=(P("mem", "fsdp"), P(("mem", "fsdp"), None)),
        check_vma=False,
    )
```
